1024 devices in a mesh: row: 16 (over z_lo, core), col: 64 (over y, z_hi, x).
Axes of the slice: x: 4, y: 8, z: 16 (z_hi: 2, z_lo: 8; z = z_hi * 8 + z_lo), core: 2. Of those that a mesh axis runs over, the one named last changes fastest.
Arguments:
- vectors: float32 [8192, 16384], P('row', 'col'), may hold values from -6 to 6
- reflectors: float32 [4, 8192, 256], P(None, ('row', 'col')), may hold values from -6 to 6
- owner_list: int32 [128], replicated, may hold values from 0 to 63, as said below
- slot_list: int32 [128], replicated, may hold values from 0 to 1
Outputs:
- result: float32 [8192, 16384], P('row', 'col')
The draws below stay inside these ranges and needn't reach their ends.
Inputs may be any that keep to these rules, and one draw needn't show every extreme that they name: owner_list * 2 + slot_list takes each value 0 to 127 exactly once.
All inputs are finite; a program needn't handle non-finite values.
Results may differ from the reference program's by a relative error of at most 0.0001.
Values sent between devices are 32-bit elements; how exact they have to be, the bound alone decides.
A program may use at most 64 MiB of HBM per device.

```python
import jax
import jax.numpy as jnp
from jax import lax

BW = 128
BLK_DEV = 2
NB = 256
PANELS = 4
NROWS = 8192
BLOCKS = 128
NCOLS = 16384


def block_order(key):
    return jax.random.permutation(jax.random.fold_in(key, 7), BLOCKS).astype(jnp.int32)


def draw_owner_list(key, part):
    return block_order(key) // BLK_DEV


def draw_slot_list(key, part):
    return block_order(key) % BLK_DEV


def level_of(key, dims, cuts, least, top_value):
    def one(axis_at, parts):
        heights = jax.random.uniform(jax.random.fold_in(jax.random.fold_in(key, 6), axis_at), (parts,), jnp.float32, least / len(cuts), top_value / len(cuts))
        return jnp.repeat(jnp.exp(heights), dims[axis_at] // parts).reshape((-1,) + (1,) * (len(dims) - axis_at - 1))

    factor_of = one(*cuts[0])
    for cut in cuts[1:]:
        factor_of = factor_of * one(*cut)
    return factor_of


def normal_values(own_key, dims, spread, reach, cuts=(), kind=jnp.bfloat16):
    array = spread * jax.random.normal(own_key, dims, jnp.float32)
    if cuts:
        array = array * level_of(own_key, dims, cuts, -0.22, 0.18)
    return jnp.clip(array, -reach, reach).astype(kind)


def setup_inputs(seed: int = 0) -> dict:
    arg_keys = jax.random.split(jax.random.key(seed), 5)
    return {
        "vectors": normal_values(arg_keys[0], (NROWS, NCOLS), 1.0, 6.0, ((0, 16), (1, 64)), jnp.float32),
        "reflectors": normal_values(arg_keys[1], (PANELS, NROWS, NB), 1.0, 6.0, ((1, 1024),), jnp.float32),
        "owner_list": draw_owner_list(jax.random.fold_in(arg_keys[4], 71), 0),
        "slot_list": draw_slot_list(jax.random.fold_in(arg_keys[4], 71), 0),
    }


def reorder(vectors, owner_list, slot_list):
    blocks = owner_list.shape[0]
    target = (owner_list * BLK_DEV + slot_list).astype(jnp.int32)
    inverse = jnp.zeros((blocks,), jnp.int32).at[target].set(jnp.arange(blocks, dtype=jnp.int32))
    blocks_view = vectors.reshape(vectors.shape[0], blocks, BW)
    return jnp.take(blocks_view, inverse, axis=1).reshape(vectors.shape[0], blocks * BW)

def apply_panel(slab_now, panel_rows, gram_sum):
    upper_form = jnp.triu(gram_sum, 1) + jnp.diag(jnp.diagonal(gram_sum) * 0.5)
    product = jnp.dot(panel_rows.T.astype(jnp.float32), slab_now.astype(jnp.float32), precision=lax.Precision.HIGHEST, preferred_element_type=jnp.float32)
    coefficients = lax.linalg.triangular_solve(upper_form, product, left_side=True, lower=False)
    return slab_now - jnp.dot(panel_rows.astype(jnp.float32), coefficients.astype(jnp.float32), precision=lax.Precision.HIGHEST, preferred_element_type=jnp.float32)

def reference(vectors, reflectors, owner_list, slot_list):
    slab_now = reorder(vectors, owner_list, slot_list)
    for panel_index in reversed(range(PANELS)):
        panel_rows = reflectors[panel_index]
        gram_sum = jnp.dot(panel_rows.T.astype(jnp.float32), panel_rows.astype(jnp.float32), precision=lax.Precision.HIGHEST, preferred_element_type=jnp.float32)
        slab_now = apply_panel(slab_now, panel_rows, gram_sum)
    return slab_now
```

```python
import functools

import jax
import jax.numpy as jnp
from jax import lax
from jax.experimental import pallas as pl
from jax.experimental.pallas import tpu as pltpu
from jax.sharding import PartitionSpec as P

BW = 128
BLK_DEV = 2
PANELS = 4
NY, NZH, NX = 8, 2, 4
CHIPS = 8
MESH = pl.DeviceIdType.MESH


def contract(left, right, left_dim, right_dim):
    return lax.dot_general(
        left,
        right,
        (((left_dim,), (right_dim,)), ((), ())),
        precision=lax.Precision.HIGHEST,
        preferred_element_type=jnp.float32,
    )


def matmul(left, right):
    return jnp.matmul(left, right, precision=lax.Precision.HIGHEST, preferred_element_type=jnp.float32)


def gather_kernel(pair, x_ref, o_ref, send_sem, recv_sem):
    row = lax.axis_index("row")
    col = lax.axis_index("col")
    core = lax.rem(row, 2)
    partner = row + 1 - 2 * core
    y = col // (NZH * NX)
    zh = lax.rem(col // NX, NZH)
    x = lax.rem(col, NX)
    half = x_ref.shape[-1] // 2

    def device(yy, zz, xx):
        return (row, (yy * NZH + zz) * NX + xx)

    up_y, down_y = lax.rem(y + 1, NY), lax.rem(y + NY - 1, NY)
    up_x, down_x = lax.rem(x + 1, NX), lax.rem(x + NX - 1, NX)
    across = device(y, 1 - zh, x)
    greeted = [device(up_y, zh, x), device(down_y, zh, x), device(y, zh, up_x), device(y, zh, down_x), across]
    if pair:
        greeted.append((partner, col))
    barrier = pltpu.get_barrier_semaphore()
    for other in greeted:
        pl.semaphore_signal(barrier, inc=1, device_id=other, device_id_type=MESH)
    pl.semaphore_wait(barrier, len(greeted))

    def spot(yy, zz, xx, h):
        lanes = slice(None) if h is None else pl.ds(h * half, half)
        middle = (core,) if pair else ()
        return o_ref.at[(yy, zz, xx) + middle + (slice(None), lanes)]

    sent = []
    counter = [0]

    def launch(source, target, number, to):
        copy = pltpu.make_async_remote_copy(
            src_ref=source,
            dst_ref=target,
            send_sem=send_sem.at[number],
            recv_sem=recv_sem.at[number],
            device_id=to,
            device_id_type=MESH,
        )
        copy.start()
        sent.append(copy)

    def arrived(target, number, origin):
        pltpu.make_async_remote_copy(
            src_ref=target,
            dst_ref=target,
            send_sem=send_sem.at[number],
            recv_sem=recv_sem.at[number],
            device_id=origin,
            device_id_type=MESH,
        ).wait_recv()

    def number():
        counter[0] += 1
        return counter[0] - 1

    everything = slice(None)

    def ring(length, place, region, first, to_device, flip):
        sign = -1 if flip else 1
        pending = []
        for hop in range(1, length // 2 + 1):
            for origin_at, origin_number, origin_from in pending:
                arrived(origin_at, origin_number, origin_from)
            pending = []
            for way in (1, -1):
                if way == -1 and hop == length // 2:
                    continue
                step = way * sign
                ahead = lax.rem(place + step + length, length)
                behind = lax.rem(place - step + length, length)
                carried = lax.rem(place - step * (hop - 1) + length * 4, length)
                coming = lax.rem(place - step * hop + length * 4, length)
                mark = number()
                source = first if (hop == 1 and first is not None) else region(carried)
                launch(source, region(carried), mark, to_device(ahead))
                pending.append((region(coming), mark, to_device(behind)))
            yield
        for origin_at, origin_number, origin_from in pending:
            arrived(origin_at, origin_number, origin_from)

    def stream(h, zz, own):
        lanes = pl.ds(h * half, half)
        first = x_ref.at[:, lanes] if own else None
        x_device = lambda p: device(y, zh, p)
        y_device = lambda p: device(p, zh, x)
        if h == 0:
            yield from ring(NX, x, lambda p: spot(y, zz, p, h), first, x_device, False)
            yield from ring(NY, y, lambda p: spot(p, zz, everything, h), None, y_device, False)
        else:
            yield from ring(NY, y, lambda p: spot(p, zz, x, h), first, y_device, True)
            yield from ring(NX, x, lambda p: spot(everything, zz, p, h), None, x_device, True)

    mark_across = number()
    launch(x_ref, spot(y, zh, x, None), mark_across, across)
    early = [stream(0, zh, True), stream(1, zh, True)]
    late = [stream(0, 1 - zh, False), stream(1, 1 - zh, False)]

    def advance(streams):
        for one in streams:
            next(one, None)

    advance(early)
    if pair:
        o_ref[y, zh, x, core] = x_ref[...]
    else:
        o_ref[y, zh, x] = x_ref[...]
    for _ in range(3):
        advance(early)
    arrived(spot(y, 1 - zh, x, None), mark_across, across)
    advance(late)
    advance(early)
    advance(late)
    advance(early)
    advance(late)
    advance(early)
    for _ in range(4):
        advance(late)
    if pair:
        mark_pair = number()
        launch(o_ref.at[:, :, :, core], o_ref.at[:, :, :, core], mark_pair, (partner, col))
        other = o_ref.at[:, :, :, 1 - core]
        arrived(other, mark_pair, (partner, col))
    for copy in sent:
        copy.wait_send()


def gather_col(block, pair, collective_id):
    rows, lanes = block.shape
    shape = (NY, NZH, NX) + ((2,) if pair else ()) + (rows, lanes)
    copies = 1 + 4 * (NX - 1 + NY - 1) + (1 if pair else 0)
    return pl.pallas_call(
        functools.partial(gather_kernel, pair),
        out_shape=jax.ShapeDtypeStruct(shape, block.dtype),
        in_specs=[pl.BlockSpec(memory_space=pltpu.VMEM)],
        out_specs=pl.BlockSpec(memory_space=pltpu.VMEM),
        scratch_shapes=[pltpu.SemaphoreType.DMA((copies,)), pltpu.SemaphoreType.DMA((copies,))],
        compiler_params=pltpu.CompilerParams(collective_id=collective_id, has_side_effects=True),
        name="gather_pair" if pair else "gather_rows",
    )(block)


def reduce_kernel(pair, subs, x_ref, o_ref, acc, from_left, from_right, swap, ssem, rsem):
    row = lax.axis_index("row")
    col = lax.axis_index("col")
    core = lax.rem(row, 2)
    me = row // 2
    partner = (row + 1 - 2 * core, col)
    right = (jnp.minimum(row + 2, 2 * CHIPS - 2 + core), col)
    left = (jnp.maximum(row - 2, core), col)
    has_left, has_right = me > 0, me < CHIPS - 1
    rows, lanes = acc.shape
    by_rows = rows >= 8 * CHIPS
    piece = rows // CHIPS // subs if by_rows else lanes // CHIPS // subs

    def part(j, q):
        start = (j * subs + q) * piece
        if by_rows:
            return (pl.ds(pl.multiple_of(start, 8), piece), slice(None))
        return (slice(None), pl.ds(pl.multiple_of(start, 128), piece))

    barrier = pltpu.get_barrier_semaphore()
    pl.semaphore_signal(barrier, inc=1, device_id=partner, device_id_type=MESH)

    @pl.when(has_left)
    def _():
        pl.semaphore_signal(barrier, inc=1, device_id=left, device_id_type=MESH)

    @pl.when(has_right)
    def _():
        pl.semaphore_signal(barrier, inc=1, device_id=right, device_id_type=MESH)

    pl.semaphore_wait(barrier, 1 + has_left.astype(jnp.int32) + has_right.astype(jnp.int32))

    def copy(source, target, kind, j, q, to):
        return pltpu.make_async_remote_copy(
            src_ref=source,
            dst_ref=target,
            send_sem=ssem.at[kind, j, q],
            recv_sem=rsem.at[kind, j, q],
            device_id=to,
            device_id_type=MESH,
        )

    def swap_copy(j, q):
        return copy(x_ref.at[(1 - core,) + part(j, q)], swap.at[part(j, q)], 0, j, q, partner)

    def rightward(j, q):
        return copy(from_left.at[part(j, q)], from_left.at[part(j, q)], 1, j, q, right)

    def leftward(j, q):
        return copy(from_right.at[part(j, q)], from_right.at[part(j, q)], 2, j, q, left)

    def out_right(j, q):
        return copy(o_at(j, q), o_at(j, q), 3, j, q, right)

    def out_left(j, q):
        return copy(o_at(j, q), o_at(j, q), 4, j, q, left)

    def out_pair(j, q):
        return copy(o_at(j, q), o_at(j, q), 5, j, q, partner)

    def other_pair(j, q):
        there = o_ref.at[(1 - core,) + part(j, q)]
        return copy(there, there, 5, j, q, partner)

    def o_at(j, q):
        return o_ref.at[(core,) + part(j, q)] if pair else o_ref.at[part(j, q)]

    order = []
    for k in range(CHIPS // 2):
        order += [CHIPS - 1 - k, k]
    for j in order:
        for q in range(subs):
            swap_copy(j, q).start()
    for j in order:
        for q in range(subs):
            swap_copy(j, q).wait_recv()
            at = part(j, q)
            acc[at] = x_ref[(core,) + at] + swap[at]

    def inward(s, _):
        for q in range(subs):

            @pl.when(jnp.logical_and(s >= me, has_right))
            def _():
                j = me + CHIPS - 1 - s
                at = part(j, q)

                @pl.when(has_left)
                def _():
                    rightward(j, q).wait_recv()
                    from_left[at] = from_left[at] + acc[at]

                @pl.when(jnp.logical_not(has_left))
                def _():
                    from_left[at] = acc[at]

                rightward(j, q).start()

            @pl.when(jnp.logical_and(s >= CHIPS - 1 - me, has_left))
            def _():
                j = me - (CHIPS - 1) + s
                at = part(j, q)

                @pl.when(has_right)
                def _():
                    leftward(j, q).wait_recv()
                    from_right[at] = from_right[at] + acc[at]

                @pl.when(jnp.logical_not(has_right))
                def _():
                    from_right[at] = acc[at]

                leftward(j, q).start()

        return 0

    lax.fori_loop(0, CHIPS - 1, inward, 0)

    for q in range(subs):
        at = part(me, q)

        @pl.when(has_left)
        def _():
            rightward(me, q).wait_recv()
            acc[at] = acc[at] + from_left[at]

        @pl.when(has_right)
        def _():
            leftward(me, q).wait_recv()
            acc[at] = acc[at] + from_right[at]

        if pair:
            o_ref[(core,) + at] = acc[at]
        else:
            o_ref[at] = acc[at]

    def outward(s, _):
        for q in range(subs):

            @pl.when(s <= me)
            def _():
                j = me - s

                @pl.when(s > 0)
                def _():
                    out_right(j, q).wait_recv()

                @pl.when(has_right)
                def _():
                    out_right(j, q).start()

                if pair:
                    out_pair(j, q).start()

            @pl.when(s <= CHIPS - 1 - me)
            def _():
                j = me + s

                @pl.when(s > 0)
                def _():
                    out_left(j, q).wait_recv()
                    if pair:
                        out_pair(j, q).start()

                @pl.when(has_left)
                def _():
                    out_left(j, q).start()

        return 0

    lax.fori_loop(0, CHIPS, outward, 0)

    def finish(j, _):
        for q in range(subs):
            swap_copy(j, q).wait_send()

            @pl.when(jnp.logical_and(has_right, j > me))
            def _():
                rightward(j, q).wait_send()

            @pl.when(jnp.logical_and(has_left, j < me))
            def _():
                leftward(j, q).wait_send()

            @pl.when(jnp.logical_and(has_right, j <= me))
            def _():
                out_right(j, q).wait_send()

            @pl.when(jnp.logical_and(has_left, j >= me))
            def _():
                out_left(j, q).wait_send()

            if pair:
                out_pair(j, q).wait_send()
                other_pair(j, q).wait_recv()
        return 0

    lax.fori_loop(0, CHIPS, finish, 0)


def reduce_row(halves, pair, subs, collective_id):
    _, rows, lanes = halves.shape
    shape = (2, rows, lanes) if pair else (rows, lanes)
    half = pltpu.VMEM((rows, lanes), halves.dtype)
    kinds = 6 if pair else 5
    return pl.pallas_call(
        functools.partial(reduce_kernel, pair, subs),
        out_shape=jax.ShapeDtypeStruct(shape, halves.dtype),
        in_specs=[pl.BlockSpec(memory_space=pltpu.VMEM)],
        out_specs=pl.BlockSpec(memory_space=pltpu.VMEM),
        scratch_shapes=[
            half,
            half,
            half,
            half,
            pltpu.SemaphoreType.DMA((kinds, CHIPS, subs)),
            pltpu.SemaphoreType.DMA((kinds, CHIPS, subs)),
        ],
        compiler_params=pltpu.CompilerParams(collective_id=collective_id, has_side_effects=True),
        name="sum_pair" if pair else "sum_half",
    )(halves)


def scaled_inverses(diag_blocks):
    order = diag_blocks.shape[-1]
    at_row = lax.broadcasted_iota(jnp.int32, (order, order), 0)
    at_col = lax.broadcasted_iota(jnp.int32, (order, order), 1)
    halves = 0.5 * jnp.sum(jnp.where(at_row == at_col, diag_blocks, 0.0), axis=2)
    strict = jnp.where(at_row < at_col, -diag_blocks / halves[:, :, None], 0.0)
    size = 16
    power = jnp.where(at_row // size == at_col // size, strict, 0.0)
    inverse = jnp.where(at_row == at_col, 1.0, power)
    for _ in range(3):
        power = matmul(power, power)
        inverse = inverse + matmul(inverse, power)
    while size < order:
        corner = jnp.where(
            jnp.logical_and(at_row // (2 * size) == at_col // (2 * size), at_row // size != at_col // size), strict, 0.0
        )
        inverse = inverse + matmul(matmul(inverse, corner), inverse)
        size *= 2
    return inverse, 1.0 / halves


def times_inverse(panel_rows, gram):
    order = gram.shape[0] // PANELS
    cut = lambda p: slice(p * order, (p + 1) * order)
    inverse, scale = scaled_inverses(jnp.stack([gram[cut(p), cut(p)] for p in range(PANELS)]))
    done = []
    for p in range(PANELS):
        rest = panel_rows[:, cut(p)]
        if p:
            rest = rest - matmul(jnp.concatenate(done, axis=1), gram[: p * order, cut(p)])
        done.append(matmul(rest, inverse[p]) * scale[p][None, :])
    return jnp.concatenate(done, axis=1)


def resort(slab_now, owner_list, slot_list):
    spread = lax.all_to_all(slab_now, "col", split_axis=0, concat_axis=1, tiled=True)
    blocks = owner_list.shape[0]
    target = owner_list * BLK_DEV + slot_list
    positions = jnp.arange(blocks, dtype=jnp.int32)
    one_hot = (target[:, None] == positions[None, :]).astype(jnp.float32)
    blocks_view = spread.reshape(spread.shape[0], blocks, BW)
    ordered = jnp.einsum(
        "rbw,bc->rcw",
        blocks_view,
        one_hot,
        precision=lax.Precision.HIGHEST,
        preferred_element_type=jnp.float32,
    )
    ordered = ordered.reshape(spread.shape[0], blocks * BW)
    return lax.all_to_all(ordered, "col", split_axis=1, concat_axis=0, tiled=True)


def on_device(vectors, reflectors, owner_list, slot_list):
    panels, rows, width = reflectors.shape
    order = panels * width
    col = lax.axis_index("col")
    own_rows = jnp.transpose(reflectors, (1, 0, 2)).reshape(rows, order)
    panel_rows = gather_col(own_rows, False, 0).reshape(NY * NZH * NX * rows, order)
    slab_now = resort(vectors, owner_list, slot_list)
    share = order // (NY * NZH * NX)
    own_columns = lax.dynamic_slice_in_dim(panel_rows, col * share, share, axis=1)
    gram_part = contract(own_columns, panel_rows, 0, 0)
    gram_half = reduce_row(gram_part.reshape(2, share // 2, order), False, 1, 1)
    gram = gather_col(gram_half, True, 2).reshape(order, order)
    product_part = contract(slab_now, panel_rows, 0, 0)
    columns = product_part.shape[0]
    product = reduce_row(product_part.reshape(2, columns // 2, order), True, 2, 3).reshape(columns, order)
    mixed = times_inverse(panel_rows, gram)
    return slab_now - contract(mixed, product, 1, 1)


def solution(mesh):
    return jax.shard_map(
        on_device,
        mesh=mesh,
        in_specs=(P("row", "col"), P(None, ("row", "col"), None), P(), P()),
        out_specs=P("row", "col"),
        check_vma=False,
    )
```

```python
import functools

import jax
import jax.numpy as jnp
from jax import lax
from jax.experimental import pallas as pl
from jax.experimental.pallas import tpu as pltpu
from jax.sharding import PartitionSpec as P

BW = 128
BLK_DEV = 2
PANELS = 4
NY, NZH, NX = 8, 2, 4
CHIPS = 8
MESH = pl.DeviceIdType.MESH
VMEM = pl.BlockSpec(memory_space=pltpu.VMEM)


def contract(left, right, left_dim, right_dim, precision=lax.Precision.HIGH):
    return lax.dot_general(
        left,
        right,
        (((left_dim,), (right_dim,)), ((), ())),
        precision=precision,
        preferred_element_type=jnp.float32,
    )


def matmul(left, right):
    return jnp.matmul(left, right, precision=lax.Precision.HIGH, preferred_element_type=jnp.float32)


def greet(always, sometimes):
    barrier = pltpu.get_barrier_semaphore()
    count = len(always)
    for other in always:
        pl.semaphore_signal(barrier, inc=1, device_id=other, device_id_type=MESH)
    for flag, other in sometimes:

        @pl.when(flag)
        def _():
            pl.semaphore_signal(barrier, inc=1, device_id=other, device_id_type=MESH)

        count = count + flag.astype(jnp.int32)
    pl.semaphore_wait(barrier, count)


def place_in_col(col):
    return col // (NZH * NX), lax.rem(col // NX, NZH), lax.rem(col, NX)


def gather_peers(row, col):
    y, zh, x = place_in_col(col)
    at = lambda yy, zz, xx: (row, (yy * NZH + zz) * NX + xx)
    peers = [at(lax.rem(y + d, NY), zh, x) for d in range(1, NY)]
    peers += [at(y, zh, lax.rem(x + d, NX)) for d in range(1, NX)]
    return peers + [at(y, 1 - zh, x)]


def gather_steps(pair, x_ref, o_ref, send_sem, recv_sem):
    row = lax.axis_index("row")
    col = lax.axis_index("col")
    core = lax.rem(row, 2)
    partner = (row + 1 - 2 * core, col)
    y, zh, x = place_in_col(col)
    quarter = x_ref.shape[-1] // 4
    lanes_of = (pl.ds(0, quarter), pl.ds(quarter, 3 * quarter))
    sent = []
    everything = slice(None)

    def device(yy, zz, xx):
        return (row, (yy * NZH + zz) * NX + xx)

    def spot(yy, zz, xx, lanes):
        middle = (core,) if pair else ()
        return o_ref.at[(yy, zz, xx) + middle + (everything, lanes)]

    def launch(source, target, to):
        number = len(sent)
        copy = pltpu.make_async_remote_copy(
            src_ref=source,
            dst_ref=target,
            send_sem=send_sem.at[number],
            recv_sem=recv_sem.at[number],
            device_id=to,
            device_id_type=MESH,
        )
        copy.start()
        sent.append(copy)
        return number

    def arrived(target, number, origin):
        pltpu.make_async_remote_copy(
            src_ref=target,
            dst_ref=target,
            send_sem=send_sem.at[number],
            recv_sem=recv_sem.at[number],
            device_id=origin,
            device_id_type=MESH,
        ).wait_recv()

    def spread(length, place, region, first, to_device):
        waits = []
        for d in sorted(range(1, length), key=lambda d: -min(d, length - d)):
            ahead = lax.rem(place + d, length)
            behind = lax.rem(place + length - d, length)
            number = launch(region(place) if first is None else first, region(place), to_device(ahead))
            waits.append((region(behind), number, to_device(behind)))
        return waits

    def finish(waits):
        for target, number, origin in waits:
            arrived(target, number, origin)

    def by_y(zz, xx, part, first):
        return spread(NY, y, lambda p: spot(p, zz, xx, lanes_of[part]), first, lambda p: device(p, zh, x))

    def by_x(zz, yy, part, first):
        return spread(NX, x, lambda p: spot(yy, zz, p, lanes_of[part]), first, lambda p: device(y, zh, p))

    whole = slice(None)
    across = launch(x_ref, spot(y, zh, x, whole), device(y, 1 - zh, x))
    near_y = by_y(zh, x, 1, x_ref.at[:, lanes_of[1]])
    near_x = by_x(zh, y, 0, x_ref.at[:, lanes_of[0]])
    if pair:
        o_ref[y, zh, x, core] = x_ref[...]
    else:
        o_ref[y, zh, x] = x_ref[...]
    yield
    finish(near_y)
    wide_x = by_x(zh, everything, 1, None)
    finish(near_x)
    wide_y = by_y(zh, everything, 0, None)
    yield
    far = 1 - zh
    arrived(spot(y, far, x, whole), across, device(y, far, x))
    far_y = by_y(far, x, 1, None)
    far_x = by_x(far, y, 0, None)
    yield
    finish(far_y)
    far_wide_x = by_x(far, everything, 1, None)
    finish(far_x)
    far_wide_y = by_y(far, everything, 0, None)
    yield
    finish(wide_x)
    finish(wide_y)

    def half_of(zz, cc):
        return o_ref.at[:, zz, :, cc]

    if pair:
        first_swap = launch(half_of(zh, core), half_of(zh, core), partner)
    yield
    finish(far_wide_x)
    finish(far_wide_y)
    if pair:
        second_swap = launch(half_of(far, core), half_of(far, core), partner)
        yield
        arrived(half_of(zh, 1 - core), first_swap, partner)
        arrived(half_of(far, 1 - core), second_swap, partner)
    for copy in sent:
        copy.wait_send()


def gather_copies(pair):
    return 1 + 4 * (NX - 1 + NY - 1) + (2 if pair else 0)


def line_places(row, col):
    core = lax.rem(row, 2)
    right = (jnp.minimum(row + 2, 2 * CHIPS - 2 + core), col)
    left = (jnp.maximum(row - 2, core), col)
    return row // 2, core, (row + 1 - 2 * core, col), left, right


def reduce_steps(subs, x_ref, o_ref, acc, from_left, from_right, swap, ssem, rsem):
    me, core, partner, left, right = line_places(lax.axis_index("row"), lax.axis_index("col"))
    has_left, has_right = me > 0, me < CHIPS - 1
    piece = acc.shape[0] // CHIPS // subs

    def part(j, q):
        return (pl.ds(pl.multiple_of((j * subs + q) * piece, 8), piece), slice(None))

    def copy(source, target, kind, j, q, to):
        return pltpu.make_async_remote_copy(
            src_ref=source,
            dst_ref=target,
            send_sem=ssem.at[kind, j, q],
            recv_sem=rsem.at[kind, j, q],
            device_id=to,
            device_id_type=MESH,
        )

    def swap_copy(j, q):
        return copy(x_ref.at[(1 - core,) + part(j, q)], swap.at[part(j, q)], 0, j, q, partner)

    def rightward(j, q):
        return copy(from_left.at[part(j, q)], from_left.at[part(j, q)], 1, j, q, right)

    def leftward(j, q):
        return copy(from_right.at[part(j, q)], from_right.at[part(j, q)], 2, j, q, left)

    def o_at(j, q):
        return o_ref.at[(core,) + part(j, q)]

    def out_right(j, q):
        return copy(o_at(j, q), o_at(j, q), 3, j, q, right)

    def out_left(j, q):
        return copy(o_at(j, q), o_at(j, q), 4, j, q, left)

    def out_pair(j, q):
        return copy(o_at(j, q), o_at(j, q), 5, j, q, partner)

    def other_pair(j, q):
        there = o_ref.at[(1 - core,) + part(j, q)]
        return copy(there, there, 5, j, q, partner)

    order = []
    for k in range(CHIPS // 2):
        order += [CHIPS - 1 - k, k]
    for j in order:
        for q in range(subs):
            swap_copy(j, q).start()
    yield
    for j in order:
        for q in range(subs):
            swap_copy(j, q).wait_recv()
            at = part(j, q)
            acc[at] = x_ref[(core,) + at] + swap[at]

    for s in range(CHIPS - 1):
        for q in range(subs):

            @pl.when(jnp.logical_and(me <= s, has_right))
            def _():
                j = me + CHIPS - 1 - s
                at = part(j, q)

                @pl.when(has_left)
                def _():
                    rightward(j, q).wait_recv()
                    from_left[at] = from_left[at] + acc[at]

                @pl.when(jnp.logical_not(has_left))
                def _():
                    from_left[at] = acc[at]

                rightward(j, q).start()

            @pl.when(jnp.logical_and(me >= CHIPS - 1 - s, has_left))
            def _():
                j = me - (CHIPS - 1) + s
                at = part(j, q)

                @pl.when(has_right)
                def _():
                    leftward(j, q).wait_recv()
                    from_right[at] = from_right[at] + acc[at]

                @pl.when(jnp.logical_not(has_right))
                def _():
                    from_right[at] = acc[at]

                leftward(j, q).start()

        yield

    for q in range(subs):
        at = part(me, q)

        @pl.when(has_left)
        def _():
            rightward(me, q).wait_recv()
            acc[at] = acc[at] + from_left[at]

        @pl.when(has_right)
        def _():
            leftward(me, q).wait_recv()
            acc[at] = acc[at] + from_right[at]

        o_ref[(core,) + at] = acc[at]

    for s in range(CHIPS):
        for q in range(subs):

            @pl.when(me >= s)
            def _():
                j = me - s
                if s:
                    out_right(j, q).wait_recv()

                @pl.when(has_right)
                def _():
                    out_right(j, q).start()

                out_pair(j, q).start()

            @pl.when(me <= CHIPS - 1 - s)
            def _():
                j = me + s
                if s:
                    out_left(j, q).wait_recv()
                    out_pair(j, q).start()

                @pl.when(has_left)
                def _():
                    out_left(j, q).start()

        yield

    def finish(j, _):
        for q in range(subs):
            swap_copy(j, q).wait_send()

            @pl.when(jnp.logical_and(has_right, j > me))
            def _():
                rightward(j, q).wait_send()

            @pl.when(jnp.logical_and(has_left, j < me))
            def _():
                leftward(j, q).wait_send()

            @pl.when(jnp.logical_and(has_right, j <= me))
            def _():
                out_right(j, q).wait_send()

            @pl.when(jnp.logical_and(has_left, j >= me))
            def _():
                out_left(j, q).wait_send()

            out_pair(j, q).wait_send()
            other_pair(j, q).wait_recv()
        return 0

    lax.fori_loop(0, CHIPS, finish, 0)


def rows_kernel(x_ref, o_ref, ssem, rsem):
    greet(gather_peers(lax.axis_index("row"), lax.axis_index("col")), [])
    for _ in gather_steps(False, x_ref, o_ref, ssem, rsem):
        pass


def short_sum_kernel(x_ref, o_ref, acc, swap, got, ssem, rsem):
    row = lax.axis_index("row")
    col = lax.axis_index("col")
    core = lax.rem(row, 2)
    me = row // 2
    partner = (row + 1 - 2 * core, col)
    on_line = lambda k: (2 * k + core, col)
    ahead = lambda d: lax.rem(me + d, CHIPS)
    behind = lambda d: lax.rem(me + CHIPS - d, CHIPS)
    lanes = acc.shape[1] // CHIPS
    chunk = lambda j: (slice(None), pl.ds(pl.multiple_of(j * lanes, lanes), lanes))
    order = list(range(1, CHIPS))
    greet([partner] + [on_line(ahead(d)) for d in order], [])

    def copy(source, target, number, to):
        return pltpu.make_async_remote_copy(
            src_ref=source,
            dst_ref=target,
            send_sem=ssem.at[number],
            recv_sem=rsem.at[number],
            device_id=to,
            device_id_type=MESH,
        )

    first = copy(x_ref.at[1 - core], swap, 0, partner)
    first.start()
    first.wait_recv()
    acc[...] = x_ref[core] + swap[...]
    inward = [copy(acc.at[chunk(ahead(d))], got.at[me], d, on_line(ahead(d))) for d in order]
    for one in inward:
        one.start()
    total = acc[chunk(me)]
    for d in order:
        there = got.at[behind(d)]
        copy(there, there, d, on_line(behind(d))).wait_recv()
        total = total + got[behind(d)]
    o_ref[chunk(me)] = total
    mine = o_ref.at[chunk(me)]
    outward = [copy(mine, mine, CHIPS - 1 + d, on_line(ahead(d))) for d in order]
    for one in outward:
        one.start()
    for d in order:
        there = o_ref.at[chunk(behind(d))]
        copy(there, there, CHIPS - 1 + d, on_line(behind(d))).wait_recv()
    for one in [first] + inward + outward:
        one.wait_send()


def joint_kernel(subs, g_ref, x_ref, gram_ref, o_ref, acc, from_left, from_right, swap, gs, gr, ssem, rsem):
    row = lax.axis_index("row")
    col = lax.axis_index("col")
    me, _, partner, left, right = line_places(row, col)
    greet(gather_peers(row, col) + [partner], [(me > 0, left), (me < CHIPS - 1, right)])
    gather = gather_steps(True, g_ref, gram_ref, gs, gr)
    reduce = reduce_steps(subs, x_ref, o_ref, acc, from_left, from_right, swap, ssem, rsem)
    for turn in "grrrgrgrrgrrrgrrrg":
        next(gather if turn == "g" else reduce, None)
    for rest in (reduce, gather):
        for _ in rest:
            pass


def cost(us):
    return pl.CostEstimate(flops=int(us * 1e9), bytes_accessed=int(us * 3e6), transcendentals=0)


def params(collective_id):
    return pltpu.CompilerParams(collective_id=collective_id, has_side_effects=True)


def dma(*shape):
    return pltpu.SemaphoreType.DMA(shape)


def gather_rows(block, collective_id):
    copies = gather_copies(False)
    return pl.pallas_call(
        rows_kernel,
        out_shape=jax.ShapeDtypeStruct((NY, NZH, NX) + block.shape, block.dtype),
        in_specs=[VMEM],
        out_specs=VMEM,
        scratch_shapes=[dma(copies), dma(copies)],
        compiler_params=params(collective_id),
        cost_estimate=cost(35),
        name="gather_rows",
    )(block)


def short_sum(halves, collective_id):
    _, rows, lanes = halves.shape
    half = pltpu.VMEM((rows, lanes), halves.dtype)
    return pl.pallas_call(
        short_sum_kernel,
        out_shape=jax.ShapeDtypeStruct((rows, lanes), halves.dtype),
        in_specs=[VMEM],
        out_specs=VMEM,
        scratch_shapes=[
            half,
            half,
            pltpu.VMEM((CHIPS, rows, lanes // CHIPS), halves.dtype),
            dma(2 * CHIPS - 1),
            dma(2 * CHIPS - 1),
        ],
        compiler_params=params(collective_id),
        cost_estimate=cost(20),
        name="short_sum",
    )(halves)


def joint(gram_half, halves, subs, collective_id):
    _, rows, lanes = halves.shape
    half = pltpu.VMEM((rows, lanes), halves.dtype)
    copies = gather_copies(True)
    return pl.pallas_call(
        functools.partial(joint_kernel, subs),
        out_shape=(
            jax.ShapeDtypeStruct((NY, NZH, NX, 2) + gram_half.shape, gram_half.dtype),
            jax.ShapeDtypeStruct(halves.shape, halves.dtype),
        ),
        in_specs=[VMEM, VMEM],
        out_specs=(VMEM, VMEM),
        scratch_shapes=[half] * 4 + [dma(copies), dma(copies), dma(6, CHIPS, subs), dma(6, CHIPS, subs)],
        compiler_params=params(collective_id),
        cost_estimate=cost(55),
        name="gram_and_sum",
    )(gram_half, halves)


def scaled_inverses(diag_blocks):
    order = diag_blocks.shape[-1]
    at_row = lax.broadcasted_iota(jnp.int32, (order, order), 0)
    at_col = lax.broadcasted_iota(jnp.int32, (order, order), 1)
    halves = 0.5 * jnp.sum(jnp.where(at_row == at_col, diag_blocks, 0.0), axis=2)
    strict = jnp.where(at_row < at_col, -diag_blocks / halves[:, :, None], 0.0)
    size = 16
    power = jnp.where(at_row // size == at_col // size, strict, 0.0)
    inverse = jnp.where(at_row == at_col, 1.0, power)
    for _ in range(3):
        power = matmul(power, power)
        inverse = inverse + matmul(inverse, power)
    while size < order:
        corner = jnp.where(
            jnp.logical_and(at_row // (2 * size) == at_col // (2 * size), at_row // size != at_col // size), strict, 0.0
        )
        inverse = inverse + matmul(matmul(inverse, corner), inverse)
        size *= 2
    return inverse, 1.0 / halves


def solve_turned(gram, product):
    order = gram.shape[0] // PANELS
    cut = lambda p: slice(p * order, (p + 1) * order)
    inverse, scale = scaled_inverses(jnp.stack([gram[cut(p), cut(p)] for p in range(PANELS)]))
    done = None
    for p in reversed(range(PANELS)):
        rest = product[:, cut(p)]
        if done is not None:
            rest = rest - contract(done, gram[cut(p), (p + 1) * order :], 1, 1)
        here = contract(rest * scale[p][None, :], inverse[p], 1, 1)
        done = here if done is None else jnp.concatenate([here, done], axis=1)
    return done


def permute_blocks(spread, owner_list, slot_list):
    blocks = owner_list.shape[0]
    target = owner_list * BLK_DEV + slot_list
    positions = jnp.arange(blocks, dtype=jnp.int32)
    one_hot = (target[:, None] == positions[None, :]).astype(jnp.float32)
    ordered = jnp.einsum(
        "rbw,bc->rcw",
        spread.reshape(spread.shape[0], blocks, BW),
        one_hot,
        precision=lax.Precision.HIGHEST,
        preferred_element_type=jnp.float32,
    )
    return ordered.reshape(spread.shape[0], blocks * BW)


def on_device(vectors, reflectors, owner_list, slot_list):
    panels, rows, width = reflectors.shape
    order = panels * width
    col = lax.axis_index("col")
    spread = lax.all_to_all(vectors, "col", split_axis=0, concat_axis=1, tiled=True)
    own_rows = jnp.transpose(reflectors, (1, 0, 2)).reshape(rows, order)
    panel_rows = gather_rows(own_rows, 0).reshape(NY * NZH * NX * rows, order)
    ordered = permute_blocks(spread, owner_list, slot_list)
    panel_rows, ordered = lax.optimization_barrier((panel_rows, ordered))
    slab_now = lax.all_to_all(ordered, "col", split_axis=1, concat_axis=0, tiled=True)
    share = order // (NY * NZH * NX)
    own_columns = lax.dynamic_slice_in_dim(panel_rows, col * share, share, axis=1)
    gram_part = contract(own_columns, panel_rows, 0, 0, lax.Precision.HIGHEST)
    gram_half = short_sum(gram_part.reshape(2, share // 2, order), 1)
    product_part = contract(slab_now, panel_rows, 0, 0)
    columns = product_part.shape[0]
    gram, product = joint(gram_half, product_part.reshape(2, columns // 2, order), 2, 2)
    turned = solve_turned(gram.reshape(order, order), product.reshape(columns, order))
    return slab_now - contract(panel_rows, turned, 1, 1)


def solution(mesh):
    return jax.shard_map(
        on_device,
        mesh=mesh,
        in_specs=(P("row", "col"), P(None, ("row", "col"), None), P(), P()),
        out_specs=P("row", "col"),
        check_vma=False,
    )
```

```python
import functools

import jax
import jax.numpy as jnp
from jax import lax
from jax.experimental import pallas as pl
from jax.experimental.pallas import tpu as pltpu
from jax.sharding import PartitionSpec as P

BW = 128
BLK_DEV = 2
PANELS = 4
NY, NZH, NX = 8, 2, 4
CHIPS = 8
MESH = pl.DeviceIdType.MESH
VMEM = pl.BlockSpec(memory_space=pltpu.VMEM)


def contract(left, right, left_dim, right_dim, precision=lax.Precision.HIGH):
    return lax.dot_general(
        left,
        right,
        (((left_dim,), (right_dim,)), ((), ())),
        precision=precision,
        preferred_element_type=jnp.float32,
    )


def matmul(left, right):
    return jnp.matmul(left, right, precision=lax.Precision.HIGH, preferred_element_type=jnp.float32)


def greet(always, sometimes):
    barrier = pltpu.get_barrier_semaphore()
    count = len(always)
    for other in always:
        pl.semaphore_signal(barrier, inc=1, device_id=other, device_id_type=MESH)
    for flag, other in sometimes:

        @pl.when(flag)
        def _():
            pl.semaphore_signal(barrier, inc=1, device_id=other, device_id_type=MESH)

        count = count + flag.astype(jnp.int32)
    pl.semaphore_wait(barrier, count)


def place_in_col(col):
    return col // (NZH * NX), lax.rem(col // NX, NZH), lax.rem(col, NX)


def gather_peers(row, col):
    y, zh, x = place_in_col(col)
    at = lambda yy, zz, xx: (row, (yy * NZH + zz) * NX + xx)
    peers = [at(lax.rem(y + d, NY), zh, x) for d in range(1, NY)]
    peers += [at(y, zh, lax.rem(x + d, NX)) for d in range(1, NX)]
    return peers + [at(y, 1 - zh, x)]


def gather_steps(pair, x_ref, o_ref, send_sem, recv_sem):
    row = lax.axis_index("row")
    col = lax.axis_index("col")
    core = lax.rem(row, 2)
    partner = (row + 1 - 2 * core, col)
    y, zh, x = place_in_col(col)
    quarter = x_ref.shape[-1] // 4
    lanes_of = (pl.ds(0, quarter), pl.ds(quarter, 3 * quarter))
    sent = []
    everything = slice(None)

    def device(yy, zz, xx):
        return (row, (yy * NZH + zz) * NX + xx)

    def spot(yy, zz, xx, lanes):
        middle = (core,) if pair else ()
        return o_ref.at[(yy, zz, xx) + middle + (everything, lanes)]

    def launch(source, target, to):
        number = len(sent)
        copy = pltpu.make_async_remote_copy(
            src_ref=source,
            dst_ref=target,
            send_sem=send_sem.at[number],
            recv_sem=recv_sem.at[number],
            device_id=to,
            device_id_type=MESH,
        )
        copy.start()
        sent.append(copy)
        return number

    def arrived(target, number, origin):
        pltpu.make_async_remote_copy(
            src_ref=target,
            dst_ref=target,
            send_sem=send_sem.at[number],
            recv_sem=recv_sem.at[number],
            device_id=origin,
            device_id_type=MESH,
        ).wait_recv()

    def spread(length, place, region, first, to_device):
        waits = []
        for d in sorted(range(1, length), key=lambda d: -min(d, length - d)):
            ahead = lax.rem(place + d, length)
            behind = lax.rem(place + length - d, length)
            number = launch(region(place) if first is None else first, region(place), to_device(ahead))
            waits.append((region(behind), number, to_device(behind)))
        return waits

    def finish(waits):
        for target, number, origin in waits:
            arrived(target, number, origin)

    def by_y(zz, xx, part, first):
        return spread(NY, y, lambda p: spot(p, zz, xx, lanes_of[part]), first, lambda p: device(p, zh, x))

    def by_x(zz, yy, part, first):
        return spread(NX, x, lambda p: spot(yy, zz, p, lanes_of[part]), first, lambda p: device(y, zh, p))

    whole = slice(None)
    across = launch(x_ref, spot(y, zh, x, whole), device(y, 1 - zh, x))
    near_y = by_y(zh, x, 1, x_ref.at[:, lanes_of[1]])
    near_x = by_x(zh, y, 0, x_ref.at[:, lanes_of[0]])
    if pair:
        o_ref[y, zh, x, core] = x_ref[...]
    else:
        o_ref[y, zh, x] = x_ref[...]
    yield
    finish(near_y)
    wide_x = by_x(zh, everything, 1, None)
    finish(near_x)
    wide_y = by_y(zh, everything, 0, None)
    yield
    far = 1 - zh
    arrived(spot(y, far, x, whole), across, device(y, far, x))
    far_y = by_y(far, x, 1, None)
    far_x = by_x(far, y, 0, None)
    yield
    finish(far_y)
    far_wide_x = by_x(far, everything, 1, None)
    finish(far_x)
    far_wide_y = by_y(far, everything, 0, None)
    yield
    finish(wide_x)
    finish(wide_y)

    def half_of(zz, cc):
        return o_ref.at[:, zz, :, cc]

    if pair:
        first_swap = launch(half_of(zh, core), half_of(zh, core), partner)
    yield
    finish(far_wide_x)
    finish(far_wide_y)
    if pair:
        second_swap = launch(half_of(far, core), half_of(far, core), partner)
        yield
        arrived(half_of(zh, 1 - core), first_swap, partner)
        arrived(half_of(far, 1 - core), second_swap, partner)
    for copy in sent:
        copy.wait_send()


def gather_copies(pair):
    return 1 + 4 * (NX - 1 + NY - 1) + (2 if pair else 0)


def line_places(row, col):
    core = lax.rem(row, 2)
    right = (jnp.minimum(row + 2, 2 * CHIPS - 2 + core), col)
    left = (jnp.maximum(row - 2, core), col)
    return row // 2, core, (row + 1 - 2 * core, col), left, right


def reduce_steps(subs, x_ref, o_ref, acc, from_left, from_right, swap, ssem, rsem):
    me, core, partner, left, right = line_places(lax.axis_index("row"), lax.axis_index("col"))
    has_left, has_right = me > 0, me < CHIPS - 1
    piece = acc.shape[0] // CHIPS // subs

    def part(j, q):
        return (pl.ds(pl.multiple_of((j * subs + q) * piece, 8), piece), slice(None))

    def copy(source, target, kind, j, q, to):
        return pltpu.make_async_remote_copy(
            src_ref=source,
            dst_ref=target,
            send_sem=ssem.at[kind, j, q],
            recv_sem=rsem.at[kind, j, q],
            device_id=to,
            device_id_type=MESH,
        )

    def swap_copy(j, q):
        return copy(x_ref.at[(1 - core,) + part(j, q)], swap.at[part(j, q)], 0, j, q, partner)

    def rightward(j, q):
        return copy(from_left.at[part(j, q)], from_left.at[part(j, q)], 1, j, q, right)

    def leftward(j, q):
        return copy(from_right.at[part(j, q)], from_right.at[part(j, q)], 2, j, q, left)

    def o_at(j, q):
        return o_ref.at[(core,) + part(j, q)]

    def out_right(j, q):
        return copy(o_at(j, q), o_at(j, q), 3, j, q, right)

    def out_left(j, q):
        return copy(o_at(j, q), o_at(j, q), 4, j, q, left)

    def out_pair(j, q):
        return copy(o_at(j, q), o_at(j, q), 5, j, q, partner)

    def other_pair(j, q):
        there = o_ref.at[(1 - core,) + part(j, q)]
        return copy(there, there, 5, j, q, partner)

    order = []
    for k in range(CHIPS // 2):
        order += [CHIPS - 1 - k, k]
    for j in order:
        for q in range(subs):
            swap_copy(j, q).start()
    yield
    for j in order:
        for q in range(subs):
            swap_copy(j, q).wait_recv()
            at = part(j, q)
            acc[at] = x_ref[(core,) + at] + swap[at]

    for s in range(CHIPS - 1):
        for q in range(subs):

            @pl.when(jnp.logical_and(me <= s, has_right))
            def _():
                j = me + CHIPS - 1 - s
                at = part(j, q)

                @pl.when(has_left)
                def _():
                    rightward(j, q).wait_recv()
                    from_left[at] = from_left[at] + acc[at]

                @pl.when(jnp.logical_not(has_left))
                def _():
                    from_left[at] = acc[at]

                rightward(j, q).start()

            @pl.when(jnp.logical_and(me >= CHIPS - 1 - s, has_left))
            def _():
                j = me - (CHIPS - 1) + s
                at = part(j, q)

                @pl.when(has_right)
                def _():
                    leftward(j, q).wait_recv()
                    from_right[at] = from_right[at] + acc[at]

                @pl.when(jnp.logical_not(has_right))
                def _():
                    from_right[at] = acc[at]

                leftward(j, q).start()

        yield

    for q in range(subs):
        at = part(me, q)

        @pl.when(has_left)
        def _():
            rightward(me, q).wait_recv()
            acc[at] = acc[at] + from_left[at]

        @pl.when(has_right)
        def _():
            leftward(me, q).wait_recv()
            acc[at] = acc[at] + from_right[at]

        o_ref[(core,) + at] = acc[at]

    for s in range(CHIPS):
        for q in range(subs):

            @pl.when(me >= s)
            def _():
                j = me - s
                if s:
                    out_right(j, q).wait_recv()

                @pl.when(has_right)
                def _():
                    out_right(j, q).start()

                out_pair(j, q).start()

            @pl.when(me <= CHIPS - 1 - s)
            def _():
                j = me + s
                if s:
                    out_left(j, q).wait_recv()
                    out_pair(j, q).start()

                @pl.when(has_left)
                def _():
                    out_left(j, q).start()

        yield

    def finish(j, _):
        for q in range(subs):
            swap_copy(j, q).wait_send()

            @pl.when(jnp.logical_and(has_right, j > me))
            def _():
                rightward(j, q).wait_send()

            @pl.when(jnp.logical_and(has_left, j < me))
            def _():
                leftward(j, q).wait_send()

            @pl.when(jnp.logical_and(has_right, j <= me))
            def _():
                out_right(j, q).wait_send()

            @pl.when(jnp.logical_and(has_left, j >= me))
            def _():
                out_left(j, q).wait_send()

            out_pair(j, q).wait_send()
            other_pair(j, q).wait_recv()
        return 0

    lax.fori_loop(0, CHIPS, finish, 0)


def resort_kernel(origin_ref, v_ref, x_ref, o_ref, s_ref, landed, ready, gs, gr, first_send, first_recv, last_send, last_recv):
    row = lax.axis_index("row")
    col = lax.axis_index("col")
    cols = NY * NZH * NX
    ahead = lambda d: lax.rem(col + d, cols)
    behind = lambda d: lax.rem(col + cols - d, cols)
    tiles = lambda c: pl.ds(BLK_DEV * c, BLK_DEV)
    barrier = pltpu.get_barrier_semaphore()

    def hello(d, _):
        pl.semaphore_signal(barrier, inc=1, device_id=(row, ahead(d)), device_id_type=MESH)
        return 0

    lax.fori_loop(1, cols, hello, 0)
    pl.semaphore_wait(barrier, cols - 1)

    def deal(source, target, d, to, send_sem, recv_sem):
        return pltpu.make_async_remote_copy(
            src_ref=source,
            dst_ref=target,
            send_sem=send_sem.at[d],
            recv_sem=recv_sem.at[d],
            device_id=(row, to),
            device_id_type=MESH,
        )

    def out(source, target, sems):
        return lambda d: deal(source.at[tiles(ahead(d))], target.at[tiles(col)], d, ahead(d), *sems)

    def coming(target, sems):
        return lambda d: deal(target.at[tiles(behind(d))], target.at[tiles(behind(d))], d, behind(d), *sems)

    first_sems, last_sems = (first_send, first_recv), (last_send, last_recv)
    first_out, first_in = out(v_ref, landed, first_sems), coming(landed, first_sems)
    last_out, last_in = out(ready, s_ref, last_sems), coming(s_ref, last_sems)

    def each(act):
        def body(d, _):
            act(d)
            return 0

        lax.fori_loop(1, cols, body, 0)

    gather = gather_steps(False, x_ref, o_ref, gs, gr)
    next(gather)
    each(lambda d: first_out(d).start())
    landed[tiles(col)] = v_ref[tiles(col)]
    for _ in range(3):
        next(gather)
    each(lambda d: first_in(d).wait_recv())

    def move(t, _):
        ready[t] = landed[origin_ref[t]]
        return 0

    lax.fori_loop(0, BLK_DEV * cols, move, 0)
    each(lambda d: last_out(d).start())
    s_ref[tiles(col)] = ready[tiles(col)]
    for _ in gather:
        pass
    each(lambda d: last_in(d).wait_recv())
    each(lambda d: first_out(d).wait_send())
    each(lambda d: last_out(d).wait_send())


def short_sum_kernel(x_ref, o_ref, acc, swap, got, ssem, rsem):
    row = lax.axis_index("row")
    col = lax.axis_index("col")
    core = lax.rem(row, 2)
    me = row // 2
    partner = (row + 1 - 2 * core, col)
    on_line = lambda k: (2 * k + core, col)
    ahead = lambda d: lax.rem(me + d, CHIPS)
    behind = lambda d: lax.rem(me + CHIPS - d, CHIPS)
    lanes = acc.shape[1] // CHIPS
    chunk = lambda j: (slice(None), pl.ds(pl.multiple_of(j * lanes, lanes), lanes))
    order = list(range(1, CHIPS))
    greet([partner] + [on_line(ahead(d)) for d in order], [])

    def copy(source, target, number, to):
        return pltpu.make_async_remote_copy(
            src_ref=source,
            dst_ref=target,
            send_sem=ssem.at[number],
            recv_sem=rsem.at[number],
            device_id=to,
            device_id_type=MESH,
        )

    first = copy(x_ref.at[1 - core], swap, 0, partner)
    first.start()
    first.wait_recv()
    acc[...] = x_ref[core] + swap[...]
    inward = [copy(acc.at[chunk(ahead(d))], got.at[me], d, on_line(ahead(d))) for d in order]
    for one in inward:
        one.start()
    total = acc[chunk(me)]
    for d in order:
        there = got.at[behind(d)]
        copy(there, there, d, on_line(behind(d))).wait_recv()
        total = total + got[behind(d)]
    o_ref[chunk(me)] = total
    mine = o_ref.at[chunk(me)]
    outward = [copy(mine, mine, CHIPS - 1 + d, on_line(ahead(d))) for d in order]
    for one in outward:
        one.start()
    for d in order:
        there = o_ref.at[chunk(behind(d))]
        copy(there, there, CHIPS - 1 + d, on_line(behind(d))).wait_recv()
    for one in [first] + inward + outward:
        one.wait_send()


def joint_kernel(subs, g_ref, x_ref, gram_ref, o_ref, acc, from_left, from_right, swap, gs, gr, ssem, rsem):
    row = lax.axis_index("row")
    col = lax.axis_index("col")
    me, _, partner, left, right = line_places(row, col)
    greet(gather_peers(row, col) + [partner], [(me > 0, left), (me < CHIPS - 1, right)])
    gather = gather_steps(True, g_ref, gram_ref, gs, gr)
    reduce = reduce_steps(subs, x_ref, o_ref, acc, from_left, from_right, swap, ssem, rsem)
    for turn in "grrrgrgrrgrrrgrrrg":
        next(gather if turn == "g" else reduce, None)
    for rest in (reduce, gather):
        for _ in rest:
            pass


def cost(us):
    return pl.CostEstimate(flops=int(us * 1e9), bytes_accessed=int(us * 3e6), transcendentals=0)


def params(collective_id):
    return pltpu.CompilerParams(collective_id=collective_id, has_side_effects=True)


def dma(*shape):
    return pltpu.SemaphoreType.DMA(shape)


def resort_and_gather(origin, vectors, block, collective_id):
    copies = gather_copies(False)
    cols = NY * NZH * NX
    tile = (8, BW)
    height, width = vectors.shape
    dealt = (height // tile[0], width // BW) + tile
    flat = (dealt[0] * dealt[1],) + tile
    tiled = jnp.transpose(vectors.reshape(dealt[0], tile[0], dealt[1], BW), (0, 2, 1, 3)).reshape(flat)
    rows, slab = pl.pallas_call(
        resort_kernel,
        out_shape=(
            jax.ShapeDtypeStruct((NY, NZH, NX) + block.shape, block.dtype),
            jax.ShapeDtypeStruct(flat, vectors.dtype),
        ),
        in_specs=[pl.BlockSpec(memory_space=pltpu.SMEM), VMEM, VMEM],
        out_specs=(VMEM, VMEM),
        scratch_shapes=[pltpu.VMEM(flat, vectors.dtype)] * 2 + [dma(copies)] * 2 + [dma(cols)] * 4,
        compiler_params=params(collective_id),
        cost_estimate=cost(60),
        name="resort_and_gather",
    )(origin, tiled, block)
    slab = jnp.transpose(slab.reshape(dealt), (0, 2, 1, 3)).reshape(height, width)
    return rows.reshape(cols * block.shape[0], block.shape[1]), slab


def short_sum(halves, collective_id):
    _, rows, lanes = halves.shape
    half = pltpu.VMEM((rows, lanes), halves.dtype)
    return pl.pallas_call(
        short_sum_kernel,
        out_shape=jax.ShapeDtypeStruct((rows, lanes), halves.dtype),
        in_specs=[VMEM],
        out_specs=VMEM,
        scratch_shapes=[
            half,
            half,
            pltpu.VMEM((CHIPS, rows, lanes // CHIPS), halves.dtype),
            dma(2 * CHIPS - 1),
            dma(2 * CHIPS - 1),
        ],
        compiler_params=params(collective_id),
        cost_estimate=cost(20),
        name="short_sum",
    )(halves)


def joint(gram_half, halves, subs, collective_id):
    _, rows, lanes = halves.shape
    half = pltpu.VMEM((rows, lanes), halves.dtype)
    copies = gather_copies(True)
    return pl.pallas_call(
        functools.partial(joint_kernel, subs),
        out_shape=(
            jax.ShapeDtypeStruct((NY, NZH, NX, 2) + gram_half.shape, gram_half.dtype),
            jax.ShapeDtypeStruct(halves.shape, halves.dtype),
        ),
        in_specs=[VMEM, VMEM],
        out_specs=(VMEM, VMEM),
        scratch_shapes=[half] * 4 + [dma(copies), dma(copies), dma(6, CHIPS, subs), dma(6, CHIPS, subs)],
        compiler_params=params(collective_id),
        cost_estimate=cost(55),
        name="gram_and_sum",
    )(gram_half, halves)


def scaled_inverses(diag_blocks):
    order = diag_blocks.shape[-1]
    at_row = lax.broadcasted_iota(jnp.int32, (order, order), 0)
    at_col = lax.broadcasted_iota(jnp.int32, (order, order), 1)
    halves = 0.5 * jnp.sum(jnp.where(at_row == at_col, diag_blocks, 0.0), axis=2)
    strict = jnp.where(at_row < at_col, -diag_blocks / halves[:, :, None], 0.0)
    size = 16
    power = jnp.where(at_row // size == at_col // size, strict, 0.0)
    inverse = jnp.where(at_row == at_col, 1.0, power)
    for _ in range(3):
        power = matmul(power, power)
        inverse = inverse + matmul(inverse, power)
    while size < order:
        corner = jnp.where(
            jnp.logical_and(at_row // (2 * size) == at_col // (2 * size), at_row // size != at_col // size), strict, 0.0
        )
        inverse = inverse + matmul(matmul(inverse, corner), inverse)
        size *= 2
    return inverse, 1.0 / halves


def solve_turned(gram, product):
    order = gram.shape[0] // PANELS
    cut = lambda p: slice(p * order, (p + 1) * order)
    inverse, scale = scaled_inverses(jnp.stack([gram[cut(p), cut(p)] for p in range(PANELS)]))
    done = None
    for p in reversed(range(PANELS)):
        rest = product[:, cut(p)]
        if done is not None:
            rest = rest - contract(done, gram[cut(p), (p + 1) * order :], 1, 1)
        here = contract(rest * scale[p][None, :], inverse[p], 1, 1)
        done = here if done is None else jnp.concatenate([here, done], axis=1)
    return done


def origins(owner_list, slot_list):
    target = owner_list * BLK_DEV + slot_list
    positions = jnp.arange(target.shape[0], dtype=jnp.int32)
    return jnp.sum(jnp.where(positions[:, None] == target[None, :], positions[None, :], 0), axis=1)


def on_device(vectors, reflectors, owner_list, slot_list):
    panels, rows, width = reflectors.shape
    order = panels * width
    col = lax.axis_index("col")
    own_rows = jnp.transpose(reflectors, (1, 0, 2)).reshape(rows, order)
    panel_rows, slab_now = resort_and_gather(origins(owner_list, slot_list), vectors, own_rows, 0)
    share = order // (NY * NZH * NX)
    own_columns = lax.dynamic_slice_in_dim(panel_rows, col * share, share, axis=1)
    gram_part = contract(own_columns, panel_rows, 0, 0, lax.Precision.HIGHEST)
    gram_half = short_sum(gram_part.reshape(2, share // 2, order), 1)
    product_part = contract(slab_now, panel_rows, 0, 0)
    columns = product_part.shape[0]
    gram, product = joint(gram_half, product_part.reshape(2, columns // 2, order), 2, 2)
    turned = solve_turned(gram.reshape(order, order), product.reshape(columns, order))
    return slab_now - contract(panel_rows, turned, 1, 1)


def solution(mesh):
    return jax.shard_map(
        on_device,
        mesh=mesh,
        in_specs=(P("row", "col"), P(None, ("row", "col"), None), P(), P()),
        out_specs=P("row", "col"),
        check_vma=False,
    )
```

```python
import functools

import jax
import jax.numpy as jnp
from jax import lax
from jax.experimental import pallas as pl
from jax.experimental.pallas import tpu as pltpu
from jax.sharding import PartitionSpec as P

BW = 128
BLK_DEV = 2
PANELS = 4
NY, NZH, NX = 8, 2, 4
CHIPS = 8
MESH = pl.DeviceIdType.MESH
VMEM = pl.BlockSpec(memory_space=pltpu.VMEM)


def contract(left, right, left_dim, right_dim, precision=lax.Precision.HIGH):
    return lax.dot_general(
        left,
        right,
        (((left_dim,), (right_dim,)), ((), ())),
        precision=precision,
        preferred_element_type=jnp.float32,
    )


def matmul(left, right):
    return jnp.matmul(left, right, precision=lax.Precision.HIGH, preferred_element_type=jnp.float32)


def greet(always, sometimes):
    barrier = pltpu.get_barrier_semaphore()
    count = len(always)
    for other in always:
        pl.semaphore_signal(barrier, inc=1, device_id=other, device_id_type=MESH)
    for flag, other in sometimes:

        @pl.when(flag)
        def _():
            pl.semaphore_signal(barrier, inc=1, device_id=other, device_id_type=MESH)

        count = count + flag.astype(jnp.int32)
    pl.semaphore_wait(barrier, count)


def place_in_col(col):
    return col // (NZH * NX), lax.rem(col // NX, NZH), lax.rem(col, NX)


def gather_peers(row, col):
    y, zh, x = place_in_col(col)
    at = lambda yy, zz, xx: (row, (yy * NZH + zz) * NX + xx)
    peers = [at(lax.rem(y + d, NY), zh, x) for d in range(1, NY)]
    peers += [at(y, zh, lax.rem(x + d, NX)) for d in range(1, NX)]
    return peers + [at(y, 1 - zh, x)]


def gather_steps(pair, x_ref, o_ref, send_sem, recv_sem):
    row = lax.axis_index("row")
    col = lax.axis_index("col")
    core = lax.rem(row, 2)
    partner = (row + 1 - 2 * core, col)
    y, zh, x = place_in_col(col)
    quarter = x_ref.shape[-1] // 4
    lanes_of = (pl.ds(0, quarter), pl.ds(quarter, 3 * quarter))
    sent = []
    everything = slice(None)

    def device(yy, zz, xx):
        return (row, (yy * NZH + zz) * NX + xx)

    def spot(yy, zz, xx, lanes):
        middle = (core,) if pair else ()
        return o_ref.at[(yy, zz, xx) + middle + (everything, lanes)]

    def launch(source, target, to):
        number = len(sent)
        copy = pltpu.make_async_remote_copy(
            src_ref=source,
            dst_ref=target,
            send_sem=send_sem.at[number],
            recv_sem=recv_sem.at[number],
            device_id=to,
            device_id_type=MESH,
        )
        copy.start()
        sent.append(copy)
        return number

    def arrived(target, number, origin):
        pltpu.make_async_remote_copy(
            src_ref=target,
            dst_ref=target,
            send_sem=send_sem.at[number],
            recv_sem=recv_sem.at[number],
            device_id=origin,
            device_id_type=MESH,
        ).wait_recv()

    def spread(length, place, region, first, to_device):
        waits = []
        for d in sorted(range(1, length), key=lambda d: -min(d, length - d)):
            ahead = lax.rem(place + d, length)
            behind = lax.rem(place + length - d, length)
            number = launch(region(place) if first is None else first, region(place), to_device(ahead))
            waits.append((region(behind), number, to_device(behind)))
        return waits

    def finish(waits):
        for target, number, origin in waits:
            arrived(target, number, origin)

    def by_y(zz, xx, part, first):
        return spread(NY, y, lambda p: spot(p, zz, xx, lanes_of[part]), first, lambda p: device(p, zh, x))

    def by_x(zz, yy, part, first):
        return spread(NX, x, lambda p: spot(yy, zz, p, lanes_of[part]), first, lambda p: device(y, zh, p))

    whole = slice(None)
    across = launch(x_ref, spot(y, zh, x, whole), device(y, 1 - zh, x))
    near_y = by_y(zh, x, 1, x_ref.at[:, lanes_of[1]])
    near_x = by_x(zh, y, 0, x_ref.at[:, lanes_of[0]])
    if pair:
        o_ref[y, zh, x, core] = x_ref[...]
    else:
        o_ref[y, zh, x] = x_ref[...]
    yield
    finish(near_y)
    wide_x = by_x(zh, everything, 1, None)
    finish(near_x)
    wide_y = by_y(zh, everything, 0, None)
    yield
    far = 1 - zh
    arrived(spot(y, far, x, whole), across, device(y, far, x))
    far_y = by_y(far, x, 1, None)
    far_x = by_x(far, y, 0, None)
    yield
    finish(far_y)
    far_wide_x = by_x(far, everything, 1, None)
    finish(far_x)
    far_wide_y = by_y(far, everything, 0, None)
    yield
    finish(wide_x)
    finish(wide_y)

    def half_of(zz, cc):
        return o_ref.at[:, zz, :, cc]

    if pair:
        first_swap = launch(half_of(zh, core), half_of(zh, core), partner)
    yield
    finish(far_wide_x)
    finish(far_wide_y)
    if pair:
        second_swap = launch(half_of(far, core), half_of(far, core), partner)
        yield
        arrived(half_of(zh, 1 - core), first_swap, partner)
        arrived(half_of(far, 1 - core), second_swap, partner)
    for copy in sent:
        copy.wait_send()


def gather_copies(pair):
    return 1 + 4 * (NX - 1 + NY - 1) + (2 if pair else 0)


def line_places(row, col):
    core = lax.rem(row, 2)
    right = (jnp.minimum(row + 2, 2 * CHIPS - 2 + core), col)
    left = (jnp.maximum(row - 2, core), col)
    return row // 2, core, (row + 1 - 2 * core, col), left, right


def reduce_steps(subs, x_ref, o_ref, acc, from_left, from_right, swap, ssem, rsem):
    me, core, partner, left, right = line_places(lax.axis_index("row"), lax.axis_index("col"))
    has_left, has_right = me > 0, me < CHIPS - 1
    rows, lanes = acc.shape[0] // CHIPS, acc.shape[1] * 2 // subs
    across = subs // 2

    def part(j, q):
        start = pl.multiple_of(j * rows + q // across * (rows // 2), 8)
        return (pl.ds(start, rows // 2), pl.ds(pl.multiple_of(lax.rem(q, across) * lanes, BW), lanes))

    def each_piece(act):
        def body(q, _):
            act(q)
            return 0

        lax.fori_loop(0, subs, body, 0)

    def copy(source, target, kind, j, q, to):
        return pltpu.make_async_remote_copy(
            src_ref=source,
            dst_ref=target,
            send_sem=ssem.at[kind, j, q],
            recv_sem=rsem.at[kind, j, q],
            device_id=to,
            device_id_type=MESH,
        )

    def swap_copy(j, q):
        return copy(x_ref.at[(1 - core,) + part(j, q)], swap.at[part(j, q)], 0, j, q, partner)

    def rightward(j, q):
        return copy(from_left.at[part(j, q)], from_left.at[part(j, q)], 1, j, q, right)

    def leftward(j, q):
        return copy(from_right.at[part(j, q)], from_right.at[part(j, q)], 2, j, q, left)

    def o_at(j, q):
        return o_ref.at[(core,) + part(j, q)]

    def out_right(j, q):
        return copy(o_at(j, q), o_at(j, q), 3, j, q, right)

    def out_left(j, q):
        return copy(o_at(j, q), o_at(j, q), 4, j, q, left)

    def out_pair(j, q):
        return copy(o_at(j, q), o_at(j, q), 5, j, q, partner)

    def other_pair(j, q):
        there = o_ref.at[(1 - core,) + part(j, q)]
        return copy(there, there, 5, j, q, partner)

    order = []
    for k in range(CHIPS // 2):
        order += [CHIPS - 1 - k, k]
    for j in order:
        each_piece(lambda q: swap_copy(j, q).start())
    yield

    def join(j, q):
        swap_copy(j, q).wait_recv()
        at = part(j, q)
        acc[at] = x_ref[(core,) + at] + swap[at]

    for j in order:
        each_piece(lambda q: join(j, q))

    def inward(s, q):
        @pl.when(jnp.logical_and(me <= s, has_right))
        def _():
            j = me + CHIPS - 1 - s
            at = part(j, q)

            @pl.when(has_left)
            def _():
                rightward(j, q).wait_recv()
                from_left[at] = from_left[at] + acc[at]

            @pl.when(jnp.logical_not(has_left))
            def _():
                from_left[at] = acc[at]

            rightward(j, q).start()

        @pl.when(jnp.logical_and(me >= CHIPS - 1 - s, has_left))
        def _():
            j = me - (CHIPS - 1) + s
            at = part(j, q)

            @pl.when(has_right)
            def _():
                leftward(j, q).wait_recv()
                from_right[at] = from_right[at] + acc[at]

            @pl.when(jnp.logical_not(has_right))
            def _():
                from_right[at] = acc[at]

            leftward(j, q).start()

    for s in range(CHIPS - 1):
        each_piece(lambda q: inward(s, q))
        yield

    def settle(q):
        at = part(me, q)

        @pl.when(has_left)
        def _():
            rightward(me, q).wait_recv()
            acc[at] = acc[at] + from_left[at]

        @pl.when(has_right)
        def _():
            leftward(me, q).wait_recv()
            acc[at] = acc[at] + from_right[at]

        o_ref[(core,) + at] = acc[at]

        @pl.when(has_right)
        def _():
            out_right(me, q).start()

        out_pair(me, q).start()

        @pl.when(has_left)
        def _():
            out_left(me, q).start()

    each_piece(settle)
    yield

    def outward(s, q):
        @pl.when(me >= s)
        def _():
            j = me - s
            out_right(j, q).wait_recv()

            @pl.when(has_right)
            def _():
                out_right(j, q).start()

            out_pair(j, q).start()

        @pl.when(me <= CHIPS - 1 - s)
        def _():
            j = me + s
            out_left(j, q).wait_recv()

            @pl.when(has_left)
            def _():
                out_left(j, q).start()

            out_pair(j, q).start()

    for s in range(1, CHIPS):
        each_piece(lambda q: outward(s, q))
        yield

    def finish(j, _):
        for q in range(subs):
            swap_copy(j, q).wait_send()

            @pl.when(jnp.logical_and(has_right, j > me))
            def _():
                rightward(j, q).wait_send()

            @pl.when(jnp.logical_and(has_left, j < me))
            def _():
                leftward(j, q).wait_send()

            @pl.when(jnp.logical_and(has_right, j <= me))
            def _():
                out_right(j, q).wait_send()

            @pl.when(jnp.logical_and(has_left, j >= me))
            def _():
                out_left(j, q).wait_send()

            out_pair(j, q).wait_send()
            other_pair(j, q).wait_recv()
        return 0

    lax.fori_loop(0, CHIPS, finish, 0)


def exchange(row, col, send_sem, recv_sem, source, target, started):
    cols = NY * NZH * NX
    tiles = lambda c: pl.ds(BLK_DEV * c, BLK_DEV)

    def copy(d):
        other = lax.rem(col + d, cols) if started else lax.rem(col + cols - d, cols)
        here = target.at[tiles(col if started else other)]
        return pltpu.make_async_remote_copy(
            src_ref=source.at[tiles(other)] if started else here,
            dst_ref=here,
            send_sem=send_sem.at[d],
            recv_sem=recv_sem.at[d],
            device_id=(row, other),
            device_id_type=MESH,
        )

    def each(act):
        def body(d, _):
            act(copy(d))
            return 0

        lax.fori_loop(1, cols, body, 0)

    return each


def greet_col(row, col, others):
    cols = NY * NZH * NX
    barrier = pltpu.get_barrier_semaphore()

    def hello(d, _):
        pl.semaphore_signal(barrier, inc=1, device_id=(row, lax.rem(col + d, cols)), device_id_type=MESH)
        return 0

    lax.fori_loop(1, cols, hello, 0)
    for other in others:
        pl.semaphore_signal(barrier, inc=1, device_id=other, device_id_type=MESH)
    pl.semaphore_wait(barrier, cols - 1 + len(others))


def deal_kernel(v_ref, x_ref, o_ref, landed, gs, gr, send_sem, recv_sem):
    row = lax.axis_index("row")
    col = lax.axis_index("col")
    own = pl.ds(BLK_DEV * col, BLK_DEV)
    greet_col(row, col, [])
    out = exchange(row, col, send_sem, recv_sem, v_ref, landed, True)
    coming = exchange(row, col, send_sem, recv_sem, v_ref, landed, False)
    gather = gather_steps(False, x_ref, o_ref, gs, gr)
    next(gather)
    out(lambda one: one.start())
    landed[own] = v_ref[own]
    for _ in gather:
        pass
    coming(lambda one: one.wait_recv())
    out(lambda one: one.wait_send())


def short_sum_steps(x_ref, o_ref, acc, swap, got, ssem, rsem):
    row = lax.axis_index("row")
    col = lax.axis_index("col")
    core = lax.rem(row, 2)
    me = row // 2
    partner = (row + 1 - 2 * core, col)
    on_line = lambda k: (2 * k + core, col)
    ahead = lambda d: lax.rem(me + d, CHIPS)
    behind = lambda d: lax.rem(me + CHIPS - d, CHIPS)
    lanes = acc.shape[1] // CHIPS
    chunk = lambda j: (slice(None), pl.ds(pl.multiple_of(j * lanes, lanes), lanes))
    order = list(range(1, CHIPS))

    def copy(source, target, number, to):
        return pltpu.make_async_remote_copy(
            src_ref=source,
            dst_ref=target,
            send_sem=ssem.at[number],
            recv_sem=rsem.at[number],
            device_id=to,
            device_id_type=MESH,
        )

    first = copy(x_ref.at[1 - core], swap, 0, partner)
    first.start()
    first.wait_recv()
    acc[...] = x_ref[core] + swap[...]
    inward = [copy(acc.at[chunk(ahead(d))], got.at[me], d, on_line(ahead(d))) for d in order]
    for one in inward:
        one.start()
    yield
    total = acc[chunk(me)]
    for d in order:
        there = got.at[behind(d)]
        copy(there, there, d, on_line(behind(d))).wait_recv()
        total = total + got[behind(d)]
    o_ref[chunk(me)] = total
    mine = o_ref.at[chunk(me)]
    outward = [copy(mine, mine, CHIPS - 1 + d, on_line(ahead(d))) for d in order]
    for one in outward:
        one.start()
    yield
    for d in order:
        there = o_ref.at[chunk(behind(d))]
        copy(there, there, CHIPS - 1 + d, on_line(behind(d))).wait_recv()
    for one in [first] + inward + outward:
        one.wait_send()


def return_kernel(origin_ref, landed, x_ref, s_ref, o_ref, ready, acc, swap, got, ssem, rsem, send_sem, recv_sem):
    row = lax.axis_index("row")
    col = lax.axis_index("col")
    me, core, partner, _, _ = line_places(row, col)
    own = pl.ds(BLK_DEV * col, BLK_DEV)
    greet_col(row, col, [partner] + [(2 * lax.rem(me + d, CHIPS) + core, col) for d in range(1, CHIPS)])
    short = short_sum_steps(x_ref, o_ref, acc, swap, got, ssem, rsem)
    next(short)

    def move(t, _):
        ready[t] = landed[origin_ref[t]]
        return 0

    lax.fori_loop(0, ready.shape[0], move, 0)
    out = exchange(row, col, send_sem, recv_sem, ready, s_ref, True)
    coming = exchange(row, col, send_sem, recv_sem, ready, s_ref, False)
    out(lambda one: one.start())
    s_ref[own] = ready[own]
    for _ in short:
        pass
    coming(lambda one: one.wait_recv())
    out(lambda one: one.wait_send())


def joint_kernel(subs, g_ref, x_ref, gram_ref, o_ref, acc, from_left, from_right, swap, gs, gr, ssem, rsem):
    row = lax.axis_index("row")
    col = lax.axis_index("col")
    me, _, partner, left, right = line_places(row, col)
    greet(gather_peers(row, col) + [partner], [(me > 0, left), (me < CHIPS - 1, right)])
    gather = gather_steps(True, g_ref, gram_ref, gs, gr)
    reduce = reduce_steps(subs, x_ref, o_ref, acc, from_left, from_right, swap, ssem, rsem)
    for turn in "grrrgrgrrgrrrgrrrg":
        next(gather if turn == "g" else reduce, None)
    for rest in (reduce, gather):
        for _ in rest:
            pass


def cost(us):
    return pl.CostEstimate(flops=int(us * 1e9), bytes_accessed=int(us * 3e6), transcendentals=0)


def params(collective_id):
    return pltpu.CompilerParams(collective_id=collective_id, has_side_effects=True)


def dma(*shape):
    return pltpu.SemaphoreType.DMA(shape)


def tiles_of(slab):
    height, width = slab.shape
    tiled = slab.reshape(height // 8, 8, width // BW, BW)
    return jnp.transpose(tiled, (0, 2, 1, 3)).reshape(-1, 8, BW)


def from_tiles(tiles, height, width):
    tiled = tiles.reshape(height // 8, width // BW, 8, BW)
    return jnp.transpose(tiled, (0, 2, 1, 3)).reshape(height, width)


def deal_and_gather(tiles, block, collective_id):
    copies = gather_copies(False)
    cols = NY * NZH * NX
    rows, landed = pl.pallas_call(
        deal_kernel,
        out_shape=(
            jax.ShapeDtypeStruct((NY, NZH, NX) + block.shape, block.dtype),
            jax.ShapeDtypeStruct(tiles.shape, tiles.dtype),
        ),
        in_specs=[VMEM, VMEM],
        out_specs=(VMEM, VMEM),
        scratch_shapes=[dma(copies)] * 2 + [dma(cols)] * 2,
        compiler_params=params(collective_id),
        cost_estimate=cost(40),
        name="deal_and_gather",
    )(tiles, block)
    return rows.reshape(cols * block.shape[0], block.shape[1]), landed


def return_and_sum(origin, landed, halves, collective_id):
    _, rows, lanes = halves.shape
    half = pltpu.VMEM((rows, lanes), halves.dtype)
    cols = NY * NZH * NX
    return pl.pallas_call(
        return_kernel,
        out_shape=(
            jax.ShapeDtypeStruct(landed.shape, landed.dtype),
            jax.ShapeDtypeStruct((rows, lanes), halves.dtype),
        ),
        in_specs=[pl.BlockSpec(memory_space=pltpu.SMEM), VMEM, VMEM],
        out_specs=(VMEM, VMEM),
        scratch_shapes=[
            pltpu.VMEM(landed.shape, landed.dtype),
            half,
            half,
            pltpu.VMEM((CHIPS, rows, lanes // CHIPS), halves.dtype),
            dma(2 * CHIPS - 1),
            dma(2 * CHIPS - 1),
            dma(cols),
            dma(cols),
        ],
        compiler_params=params(collective_id),
        cost_estimate=cost(35),
        name="return_and_sum",
    )(origin, landed, halves)


def joint(gram_half, halves, subs, collective_id):
    _, rows, lanes = halves.shape
    half = pltpu.VMEM((rows, lanes), halves.dtype)
    copies = gather_copies(True)
    return pl.pallas_call(
        functools.partial(joint_kernel, subs),
        out_shape=(
            jax.ShapeDtypeStruct((NY, NZH, NX, 2) + gram_half.shape, gram_half.dtype),
            jax.ShapeDtypeStruct(halves.shape, halves.dtype),
        ),
        in_specs=[VMEM, VMEM],
        out_specs=(VMEM, VMEM),
        scratch_shapes=[half] * 4 + [dma(copies), dma(copies), dma(6, CHIPS, subs), dma(6, CHIPS, subs)],
        compiler_params=params(collective_id),
        cost_estimate=cost(55),
        name="gram_and_sum",
    )(gram_half, halves)


def scaled_inverses(diag_blocks):
    order = diag_blocks.shape[-1]
    at_row = lax.broadcasted_iota(jnp.int32, (order, order), 0)
    at_col = lax.broadcasted_iota(jnp.int32, (order, order), 1)
    halves = 0.5 * jnp.sum(jnp.where(at_row == at_col, diag_blocks, 0.0), axis=2)
    strict = jnp.where(at_row < at_col, -diag_blocks / halves[:, :, None], 0.0)
    size = 16
    power = jnp.where(at_row // size == at_col // size, strict, 0.0)
    inverse = jnp.where(at_row == at_col, 1.0, power)
    for _ in range(3):
        power = matmul(power, power)
        inverse = inverse + matmul(inverse, power)
    while size < order:
        corner = jnp.where(
            jnp.logical_and(at_row // (2 * size) == at_col // (2 * size), at_row // size != at_col // size), strict, 0.0
        )
        inverse = inverse + matmul(matmul(inverse, corner), inverse)
        size *= 2
    return inverse, 1.0 / halves


def solve_turned(gram, product):
    order = gram.shape[0] // PANELS
    cut = lambda p: slice(p * order, (p + 1) * order)
    inverse, scale = scaled_inverses(jnp.stack([gram[cut(p), cut(p)] for p in range(PANELS)]))
    done = None
    for p in reversed(range(PANELS)):
        rest = product[:, cut(p)]
        if done is not None:
            rest = rest - contract(done, gram[cut(p), (p + 1) * order :], 1, 1)
        here = contract(rest * scale[p][None, :], inverse[p], 1, 1)
        done = here if done is None else jnp.concatenate([here, done], axis=1)
    return done


def origins(owner_list, slot_list):
    target = owner_list * BLK_DEV + slot_list
    positions = jnp.arange(target.shape[0], dtype=jnp.int32)
    return jnp.sum(jnp.where(positions[:, None] == target[None, :], positions[None, :], 0), axis=1)


def on_device(vectors, reflectors, owner_list, slot_list):
    panels, rows, width = reflectors.shape
    order = panels * width
    col = lax.axis_index("col")
    own_rows = jnp.transpose(reflectors, (1, 0, 2)).reshape(rows, order)
    panel_rows, landed = deal_and_gather(tiles_of(vectors), own_rows, 0)
    share = order // (NY * NZH * NX)
    own_columns = lax.dynamic_slice_in_dim(panel_rows, col * share, share, axis=1)
    gram_part = contract(own_columns, panel_rows, 0, 0, lax.Precision.HIGHEST)
    origin = origins(owner_list, slot_list)
    tiles, gram_half = return_and_sum(origin, landed, gram_part.reshape(2, share // 2, order), 1)
    slab_now = from_tiles(tiles, *vectors.shape)
    product_part = contract(slab_now, panel_rows, 0, 0)
    columns = product_part.shape[0]
    gram, product = joint(gram_half, product_part.reshape(2, columns // 2, order), 4, 2)
    turned = solve_turned(gram.reshape(order, order), product.reshape(columns, order))
    return slab_now - contract(panel_rows, turned, 1, 1)


def solution(mesh):
    return jax.shard_map(
        on_device,
        mesh=mesh,
        in_specs=(P("row", "col"), P(None, ("row", "col"), None), P(), P()),
        out_specs=P("row", "col"),
        check_vma=False,
    )
```

```python
import functools

import jax
import jax.numpy as jnp
from jax import lax
from jax.experimental import pallas as pl
from jax.experimental.pallas import tpu as pltpu
from jax.sharding import PartitionSpec as P

BW = 128
BLK_DEV = 2
PANELS = 4
NY, NZH, NX = 8, 2, 4
CHIPS = 8
MESH = pl.DeviceIdType.MESH
VMEM = pl.BlockSpec(memory_space=pltpu.VMEM)


def contract(left, right, left_dim, right_dim, precision=lax.Precision.HIGH):
    return lax.dot_general(
        left,
        right,
        (((left_dim,), (right_dim,)), ((), ())),
        precision=precision,
        preferred_element_type=jnp.float32,
    )


def matmul(left, right):
    return jnp.matmul(left, right, precision=lax.Precision.HIGH, preferred_element_type=jnp.float32)


def greet(always, sometimes):
    barrier = pltpu.get_barrier_semaphore()
    count = len(always)
    for other in always:
        pl.semaphore_signal(barrier, inc=1, device_id=other, device_id_type=MESH)
    for flag, other in sometimes:

        @pl.when(flag)
        def _():
            pl.semaphore_signal(barrier, inc=1, device_id=other, device_id_type=MESH)

        count = count + flag.astype(jnp.int32)
    pl.semaphore_wait(barrier, count)


def place_in_col(col):
    return col // (NZH * NX), lax.rem(col // NX, NZH), lax.rem(col, NX)


def gather_peers(row, col):
    y, zh, x = place_in_col(col)
    at = lambda yy, zz, xx: (row, (yy * NZH + zz) * NX + xx)
    peers = [at(lax.rem(y + d, NY), zh, x) for d in range(1, NY)]
    peers += [at(y, zh, lax.rem(x + d, NX)) for d in range(1, NX)]
    return peers + [at(y, 1 - zh, x)]


def gather_steps(pair, x_ref, o_ref, send_sem, recv_sem):
    row = lax.axis_index("row")
    col = lax.axis_index("col")
    core = lax.rem(row, 2)
    partner = (row + 1 - 2 * core, col)
    y, zh, x = place_in_col(col)
    quarter = x_ref.shape[-1] // 4
    lanes_of = (pl.ds(0, quarter), pl.ds(quarter, 3 * quarter))
    sent = []
    everything = slice(None)

    def device(yy, zz, xx):
        return (row, (yy * NZH + zz) * NX + xx)

    def spot(yy, zz, xx, lanes):
        middle = (core,) if pair else ()
        return o_ref.at[(yy, zz, xx) + middle + (everything, lanes)]

    def launch(source, target, to):
        number = len(sent)
        copy = pltpu.make_async_remote_copy(
            src_ref=source,
            dst_ref=target,
            send_sem=send_sem.at[number],
            recv_sem=recv_sem.at[number],
            device_id=to,
            device_id_type=MESH,
        )
        copy.start()
        sent.append(copy)
        return number

    def arrived(target, number, origin):
        pltpu.make_async_remote_copy(
            src_ref=target,
            dst_ref=target,
            send_sem=send_sem.at[number],
            recv_sem=recv_sem.at[number],
            device_id=origin,
            device_id_type=MESH,
        ).wait_recv()

    def spread(length, place, region, first, to_device):
        waits = []
        for d in sorted(range(1, length), key=lambda d: -min(d, length - d)):
            ahead = lax.rem(place + d, length)
            behind = lax.rem(place + length - d, length)
            number = launch(region(place) if first is None else first, region(place), to_device(ahead))
            waits.append((region(behind), number, to_device(behind)))
        return waits

    def finish(waits):
        for target, number, origin in waits:
            arrived(target, number, origin)

    def by_y(zz, xx, part, first):
        return spread(NY, y, lambda p: spot(p, zz, xx, lanes_of[part]), first, lambda p: device(p, zh, x))

    def by_x(zz, yy, part, first):
        return spread(NX, x, lambda p: spot(yy, zz, p, lanes_of[part]), first, lambda p: device(y, zh, p))

    whole = slice(None)
    across = launch(x_ref, spot(y, zh, x, whole), device(y, 1 - zh, x))
    near_y = by_y(zh, x, 1, x_ref.at[:, lanes_of[1]])
    near_x = by_x(zh, y, 0, x_ref.at[:, lanes_of[0]])
    if pair:
        o_ref[y, zh, x, core] = x_ref[...]
    else:
        o_ref[y, zh, x] = x_ref[...]
    yield
    finish(near_y)
    wide_x = by_x(zh, everything, 1, None)
    finish(near_x)
    wide_y = by_y(zh, everything, 0, None)
    yield
    far = 1 - zh
    arrived(spot(y, far, x, whole), across, device(y, far, x))
    far_y = by_y(far, x, 1, None)
    far_x = by_x(far, y, 0, None)
    yield
    finish(far_y)
    far_wide_x = by_x(far, everything, 1, None)
    finish(far_x)
    far_wide_y = by_y(far, everything, 0, None)
    yield
    finish(wide_x)
    finish(wide_y)

    def half_of(zz, cc):
        return o_ref.at[:, zz, :, cc]

    if pair:
        first_swap = launch(half_of(zh, core), half_of(zh, core), partner)
    yield
    finish(far_wide_x)
    finish(far_wide_y)
    if pair:
        second_swap = launch(half_of(far, core), half_of(far, core), partner)
        yield
        arrived(half_of(zh, 1 - core), first_swap, partner)
        arrived(half_of(far, 1 - core), second_swap, partner)
    for copy in sent:
        copy.wait_send()


def gather_copies(pair):
    return 1 + 4 * (NX - 1 + NY - 1) + (2 if pair else 0)


def line_places(row, col):
    core = lax.rem(row, 2)
    chip = row // 2
    parity = lax.rem(chip, 2)
    right = (jnp.minimum(row + 4, 2 * CHIPS - 4 + 2 * parity + core), col)
    left = (jnp.maximum(row - 4, 2 * parity + core), col)
    return chip // 2, parity, core, (row + 1 - 2 * core, col), (row + 2 - 4 * parity, col), left, right


def reduce_steps(subs, x_ref, o_ref, acc, near, from_left, from_right, swap, ssem, rsem):
    me, parity, core, partner, mate, left, right = line_places(lax.axis_index("row"), lax.axis_index("col"))
    length = CHIPS // 2
    has_left, has_right = me > 0, me < length - 1
    piece = acc.shape[0] // CHIPS // subs
    mine = lambda b: 2 * b + parity
    others = lambda b: 2 * b + 1 - parity

    def part(j, q):
        return (pl.ds(pl.multiple_of((j * subs + q) * piece, 8), piece), slice(None))

    def copy(source, target, kind, j, q, to):
        return pltpu.make_async_remote_copy(
            src_ref=source,
            dst_ref=target,
            send_sem=ssem.at[kind, j, q],
            recv_sem=rsem.at[kind, j, q],
            device_id=to,
            device_id_type=MESH,
        )

    def here(buffer, kind, to):
        return lambda j, q: copy(buffer.at[part(j, q)], buffer.at[part(j, q)], kind, j, q, to)

    def swap_copy(j, q):
        return copy(x_ref.at[(1 - core,) + part(j, q)], swap.at[part(j, q)], 0, j, q, partner)

    def to_mate(j, q):
        return copy(acc.at[part(j, q)], near.at[part(j, q)], 1, j, q, mate)

    rightward, leftward = here(from_left, 2, right), here(from_right, 3, left)

    def out(kind, to):
        def made(j, q):
            place = o_ref.at[(core,) + part(j, q)]
            return copy(place, place, kind, j, q, to)

        return made

    out_right, out_left, out_mate, out_pair = out(4, right), out(5, left), out(6, mate), out(7, partner)

    def other_pair(j, q):
        there = o_ref.at[(1 - core,) + part(j, q)]
        return copy(there, there, 7, j, q, partner)

    def joined(j, q):
        swap_copy(j, q).wait_recv()
        at = part(j, q)
        return x_ref[(core,) + at] + swap[at]

    def with_mate(j, q):
        value = joined(j, q)
        to_mate(j, q).wait_recv()
        return value + near[part(j, q)]

    order = []
    for k in range(length // 2):
        order += [length - 1 - k, k]
    for b in order:
        for q in range(subs):
            swap_copy(others(b), q).start()
            swap_copy(mine(b), q).start()
    yield
    for b in order:
        for q in range(subs):
            acc[part(others(b), q)] = joined(others(b), q)
            to_mate(others(b), q).start()
    yield

    for s in range(length - 1):
        for q in range(subs):

            @pl.when(jnp.logical_and(me <= s, has_right))
            def _():
                j = mine(me + length - 1 - s)
                at = part(j, q)
                value = with_mate(j, q)

                @pl.when(has_left)
                def _():
                    rightward(j, q).wait_recv()
                    from_left[at] = from_left[at] + value

                @pl.when(jnp.logical_not(has_left))
                def _():
                    from_left[at] = value

                rightward(j, q).start()

            @pl.when(jnp.logical_and(me >= length - 1 - s, has_left))
            def _():
                j = mine(me - (length - 1) + s)
                at = part(j, q)
                value = with_mate(j, q)

                @pl.when(has_right)
                def _():
                    leftward(j, q).wait_recv()
                    from_right[at] = from_right[at] + value

                @pl.when(jnp.logical_not(has_right))
                def _():
                    from_right[at] = value

                leftward(j, q).start()

        yield

    for q in range(subs):
        j = mine(me)
        at = part(j, q)
        acc[at] = with_mate(j, q)

        @pl.when(has_left)
        def _():
            rightward(j, q).wait_recv()
            acc[at] = acc[at] + from_left[at]

        @pl.when(has_right)
        def _():
            leftward(j, q).wait_recv()
            acc[at] = acc[at] + from_right[at]

        o_ref[(core,) + at] = acc[at]

        @pl.when(has_right)
        def _():
            out_right(j, q).start()

        @pl.when(has_left)
        def _():
            out_left(j, q).start()

        out_mate(j, q).start()
        out_pair(j, q).start()

    yield

    def pass_on(b, q):
        out_mate(others(b), q).wait_recv()
        out_pair(others(b), q).start()

    for s in range(1, length + 1):
        for q in range(subs):
            if s < length:

                @pl.when(me >= s)
                def _():
                    j = mine(me - s)
                    out_right(j, q).wait_recv()

                    @pl.when(has_right)
                    def _():
                        out_right(j, q).start()

                    out_mate(j, q).start()
                    out_pair(j, q).start()

                @pl.when(me <= length - 1 - s)
                def _():
                    j = mine(me + s)
                    out_left(j, q).wait_recv()

                    @pl.when(has_left)
                    def _():
                        out_left(j, q).start()

                    out_mate(j, q).start()
                    out_pair(j, q).start()

            if s == 1:
                pass_on(me, q)
            else:

                @pl.when(me >= s - 1)
                def _():
                    pass_on(me - (s - 1), q)

                @pl.when(me <= length - s)
                def _():
                    pass_on(me + (s - 1), q)

        yield

    def finish(b, _):
        for q in range(subs):
            j = mine(b)
            swap_copy(j, q).wait_send()
            swap_copy(others(b), q).wait_send()
            to_mate(others(b), q).wait_send()

            @pl.when(jnp.logical_and(has_right, b > me))
            def _():
                rightward(j, q).wait_send()

            @pl.when(jnp.logical_and(has_left, b < me))
            def _():
                leftward(j, q).wait_send()

            @pl.when(jnp.logical_and(has_right, b <= me))
            def _():
                out_right(j, q).wait_send()

            @pl.when(jnp.logical_and(has_left, b >= me))
            def _():
                out_left(j, q).wait_send()

            out_mate(j, q).wait_send()
            for k in (j, others(b)):
                out_pair(k, q).wait_send()
                other_pair(k, q).wait_recv()
        return 0

    lax.fori_loop(0, length, finish, 0)


def rows_kernel(x_ref, o_ref, ssem, rsem):
    greet(gather_peers(lax.axis_index("row"), lax.axis_index("col")), [])
    for _ in gather_steps(False, x_ref, o_ref, ssem, rsem):
        pass


def short_sum_kernel(x_ref, o_ref, acc, swap, got, ssem, rsem):
    row = lax.axis_index("row")
    col = lax.axis_index("col")
    core = lax.rem(row, 2)
    me = row // 2
    partner = (row + 1 - 2 * core, col)
    on_line = lambda k: (2 * k + core, col)
    ahead = lambda d: lax.rem(me + d, CHIPS)
    behind = lambda d: lax.rem(me + CHIPS - d, CHIPS)
    lanes = acc.shape[1] // CHIPS
    chunk = lambda j: (slice(None), pl.ds(pl.multiple_of(j * lanes, lanes), lanes))
    order = list(range(1, CHIPS))
    greet([partner] + [on_line(ahead(d)) for d in order], [])

    def copy(source, target, number, to):
        return pltpu.make_async_remote_copy(
            src_ref=source,
            dst_ref=target,
            send_sem=ssem.at[number],
            recv_sem=rsem.at[number],
            device_id=to,
            device_id_type=MESH,
        )

    first = copy(x_ref.at[1 - core], swap, 0, partner)
    first.start()
    first.wait_recv()
    acc[...] = x_ref[core] + swap[...]
    inward = [copy(acc.at[chunk(ahead(d))], got.at[me], d, on_line(ahead(d))) for d in order]
    for one in inward:
        one.start()
    total = acc[chunk(me)]
    for d in order:
        there = got.at[behind(d)]
        copy(there, there, d, on_line(behind(d))).wait_recv()
        total = total + got[behind(d)]
    o_ref[chunk(me)] = total
    mine = o_ref.at[chunk(me)]
    outward = [copy(mine, mine, CHIPS - 1 + d, on_line(ahead(d))) for d in order]
    for one in outward:
        one.start()
    for d in order:
        there = o_ref.at[chunk(behind(d))]
        copy(there, there, CHIPS - 1 + d, on_line(behind(d))).wait_recv()
    for one in [first] + inward + outward:
        one.wait_send()


def joint_kernel(subs, g_ref, x_ref, gram_ref, o_ref, acc, near, from_left, from_right, swap, gs, gr, ssem, rsem):
    row = lax.axis_index("row")
    col = lax.axis_index("col")
    me, _, _, partner, mate, left, right = line_places(row, col)
    greet(gather_peers(row, col) + [partner, mate], [(me > 0, left), (me < CHIPS // 2 - 1, right)])
    gather = gather_steps(True, g_ref, gram_ref, gs, gr)
    reduce = reduce_steps(subs, x_ref, o_ref, acc, near, from_left, from_right, swap, ssem, rsem)
    for turn in "grrgrrgrgrrgrrg":
        next(gather if turn == "g" else reduce, None)
    for rest in (reduce, gather):
        for _ in rest:
            pass


def cost(us):
    return pl.CostEstimate(flops=int(us * 1e9), bytes_accessed=int(us * 3e6), transcendentals=0)


def params(collective_id):
    return pltpu.CompilerParams(collective_id=collective_id, has_side_effects=True)


def dma(*shape):
    return pltpu.SemaphoreType.DMA(shape)


def gather_rows(block, collective_id):
    copies = gather_copies(False)
    return pl.pallas_call(
        rows_kernel,
        out_shape=jax.ShapeDtypeStruct((NY, NZH, NX) + block.shape, block.dtype),
        in_specs=[VMEM],
        out_specs=VMEM,
        scratch_shapes=[dma(copies), dma(copies)],
        compiler_params=params(collective_id),
        cost_estimate=cost(35),
        name="gather_rows",
    )(block)


def short_sum(halves, collective_id):
    _, rows, lanes = halves.shape
    half = pltpu.VMEM((rows, lanes), halves.dtype)
    return pl.pallas_call(
        short_sum_kernel,
        out_shape=jax.ShapeDtypeStruct((rows, lanes), halves.dtype),
        in_specs=[VMEM],
        out_specs=VMEM,
        scratch_shapes=[
            half,
            half,
            pltpu.VMEM((CHIPS, rows, lanes // CHIPS), halves.dtype),
            dma(2 * CHIPS - 1),
            dma(2 * CHIPS - 1),
        ],
        compiler_params=params(collective_id),
        cost_estimate=cost(20),
        name="short_sum",
    )(halves)


def joint(gram_half, halves, subs, collective_id):
    _, rows, lanes = halves.shape
    half = pltpu.VMEM((rows, lanes), halves.dtype)
    copies = gather_copies(True)
    return pl.pallas_call(
        functools.partial(joint_kernel, subs),
        out_shape=(
            jax.ShapeDtypeStruct((NY, NZH, NX, 2) + gram_half.shape, gram_half.dtype),
            jax.ShapeDtypeStruct(halves.shape, halves.dtype),
        ),
        in_specs=[VMEM, VMEM],
        out_specs=(VMEM, VMEM),
        scratch_shapes=[half] * 5 + [dma(copies), dma(copies), dma(8, CHIPS, subs), dma(8, CHIPS, subs)],
        compiler_params=params(collective_id),
        cost_estimate=cost(55),
        name="gram_and_sum",
    )(gram_half, halves)


def scaled_inverses(diag_blocks):
    order = diag_blocks.shape[-1]
    at_row = lax.broadcasted_iota(jnp.int32, (order, order), 0)
    at_col = lax.broadcasted_iota(jnp.int32, (order, order), 1)
    halves = 0.5 * jnp.sum(jnp.where(at_row == at_col, diag_blocks, 0.0), axis=2)
    strict = jnp.where(at_row < at_col, -diag_blocks / halves[:, :, None], 0.0)
    size = 16
    power = jnp.where(at_row // size == at_col // size, strict, 0.0)
    inverse = jnp.where(at_row == at_col, 1.0, power)
    for _ in range(3):
        power = matmul(power, power)
        inverse = inverse + matmul(inverse, power)
    while size < order:
        corner = jnp.where(
            jnp.logical_and(at_row // (2 * size) == at_col // (2 * size), at_row // size != at_col // size), strict, 0.0
        )
        inverse = inverse + matmul(matmul(inverse, corner), inverse)
        size *= 2
    return inverse, 1.0 / halves


def solve_turned(gram, product):
    order = gram.shape[0] // PANELS
    cut = lambda p: slice(p * order, (p + 1) * order)
    inverse, scale = scaled_inverses(jnp.stack([gram[cut(p), cut(p)] for p in range(PANELS)]))
    done = None
    for p in reversed(range(PANELS)):
        rest = product[:, cut(p)]
        if done is not None:
            rest = rest - contract(done, gram[cut(p), (p + 1) * order :], 1, 1)
        here = contract(rest * scale[p][None, :], inverse[p], 1, 1)
        done = here if done is None else jnp.concatenate([here, done], axis=1)
    return done


def permute_blocks(spread, owner_list, slot_list):
    blocks = owner_list.shape[0]
    target = owner_list * BLK_DEV + slot_list
    positions = jnp.arange(blocks, dtype=jnp.int32)
    one_hot = (target[:, None] == positions[None, :]).astype(jnp.float32)
    ordered = jnp.einsum(
        "rbw,bc->rcw",
        spread.reshape(spread.shape[0], blocks, BW),
        one_hot,
        precision=lax.Precision.HIGHEST,
        preferred_element_type=jnp.float32,
    )
    return ordered.reshape(spread.shape[0], blocks * BW)


def on_device(vectors, reflectors, owner_list, slot_list):
    panels, rows, width = reflectors.shape
    order = panels * width
    col = lax.axis_index("col")
    spread = lax.all_to_all(vectors, "col", split_axis=0, concat_axis=1, tiled=True)
    own_rows = jnp.transpose(reflectors, (1, 0, 2)).reshape(rows, order)
    panel_rows = gather_rows(own_rows, 0).reshape(NY * NZH * NX * rows, order)
    ordered = permute_blocks(spread, owner_list, slot_list)
    panel_rows, ordered = lax.optimization_barrier((panel_rows, ordered))
    slab_now = lax.all_to_all(ordered, "col", split_axis=1, concat_axis=0, tiled=True)
    share = order // (NY * NZH * NX)
    own_columns = lax.dynamic_slice_in_dim(panel_rows, col * share, share, axis=1)
    gram_part = contract(own_columns, panel_rows, 0, 0, lax.Precision.HIGHEST)
    gram_half = short_sum(gram_part.reshape(2, share // 2, order), 1)
    product_part = contract(slab_now, panel_rows, 0, 0)
    columns = product_part.shape[0]
    gram, product = joint(gram_half, product_part.reshape(2, columns // 2, order), 2, 2)
    turned = solve_turned(gram.reshape(order, order), product.reshape(columns, order))
    return slab_now - contract(panel_rows, turned, 1, 1)


def solution(mesh):
    return jax.shard_map(
        on_device,
        mesh=mesh,
        in_specs=(P("row", "col"), P(None, ("row", "col"), None), P(), P()),
        out_specs=P("row", "col"),
        check_vma=False,
    )
```

```python
import functools

import jax
import jax.numpy as jnp
from jax import lax
from jax.experimental import pallas as pl
from jax.experimental.pallas import tpu as pltpu
from jax.sharding import PartitionSpec as P

BW = 128
BLK_DEV = 2
PANELS = 4
NY, NZH, NX = 8, 2, 4
CHIPS = 8
MESH = pl.DeviceIdType.MESH
VMEM = pl.BlockSpec(memory_space=pltpu.VMEM)


def contract(left, right, left_dim, right_dim, precision=lax.Precision.HIGH):
    return lax.dot_general(
        left,
        right,
        (((left_dim,), (right_dim,)), ((), ())),
        precision=precision,
        preferred_element_type=jnp.float32,
    )


def matmul(left, right):
    return jnp.matmul(left, right, precision=lax.Precision.HIGH, preferred_element_type=jnp.float32)


def greet(always, sometimes):
    barrier = pltpu.get_barrier_semaphore()
    count = len(always)
    for other in always:
        pl.semaphore_signal(barrier, inc=1, device_id=other, device_id_type=MESH)
    for flag, other in sometimes:

        @pl.when(flag)
        def _():
            pl.semaphore_signal(barrier, inc=1, device_id=other, device_id_type=MESH)

        count = count + flag.astype(jnp.int32)
    pl.semaphore_wait(barrier, count)


def place_in_col(col):
    return col // (NZH * NX), lax.rem(col // NX, NZH), lax.rem(col, NX)


def gather_peers(row, col):
    y, zh, x = place_in_col(col)
    at = lambda yy, zz, xx: (row, (yy * NZH + zz) * NX + xx)
    peers = [at(lax.rem(y + d, NY), zh, x) for d in range(1, NY)]
    peers += [at(y, zh, lax.rem(x + d, NX)) for d in range(1, NX)]
    return peers + [at(y, 1 - zh, x)]


def gather_steps(pair, x_ref, o_ref, send_sem, recv_sem):
    row = lax.axis_index("row")
    col = lax.axis_index("col")
    core = lax.rem(row, 2)
    partner = (row + 1 - 2 * core, col)
    y, zh, x = place_in_col(col)
    quarter = x_ref.shape[-1] // 4
    lanes_of = (pl.ds(0, quarter), pl.ds(quarter, 3 * quarter))
    sent = []
    everything = slice(None)

    def device(yy, zz, xx):
        return (row, (yy * NZH + zz) * NX + xx)

    def spot(yy, zz, xx, lanes, of=core):
        middle = (of,) if pair else ()
        return o_ref.at[(yy, zz, xx) + middle + (everything, lanes)]

    def launch(source, target, to):
        number = len(sent)
        copy = pltpu.make_async_remote_copy(
            src_ref=source,
            dst_ref=target,
            send_sem=send_sem.at[number],
            recv_sem=recv_sem.at[number],
            device_id=to,
            device_id_type=MESH,
        )
        copy.start()
        sent.append(copy)
        return number

    def arrived(target, number, origin):
        pltpu.make_async_remote_copy(
            src_ref=target,
            dst_ref=target,
            send_sem=send_sem.at[number],
            recv_sem=recv_sem.at[number],
            device_id=origin,
            device_id_type=MESH,
        ).wait_recv()

    def spread(length, place, region, first, to_device):
        waits = []
        for d in sorted(range(1, length), key=lambda d: -min(d, length - d)):
            ahead = lax.rem(place + d, length)
            behind = lax.rem(place + length - d, length)
            number = launch(region(place) if first is None else first, region(place), to_device(ahead))
            waits.append((region(behind), number, to_device(behind)))
        return waits

    def finish(waits):
        for target, number, origin in waits:
            arrived(target, number, origin)

    def hand_over(swaps, region, p):
        swaps.append((region(p, 1 - core), launch(region(p, core), region(p, core), partner), partner))

    def finish_and_hand(swaps, waits, length, place, region):
        for (target, number, origin), d in zip(waits, sorted(range(1, length), key=lambda d: -min(d, length - d))):
            arrived(target, number, origin)
            hand_over(swaps, region, lax.rem(place + length - d, length))

    def by_y(zz, xx, part, first):
        return spread(NY, y, lambda p: spot(p, zz, xx, lanes_of[part]), first, lambda p: device(p, zh, x))

    def by_x(zz, yy, part, first):
        return spread(NX, x, lambda p: spot(yy, zz, p, lanes_of[part]), first, lambda p: device(y, zh, p))

    whole = slice(None)
    across = launch(x_ref, spot(y, zh, x, whole), device(y, 1 - zh, x))
    near_y = by_y(zh, x, 1, x_ref.at[:, lanes_of[1]])
    near_x = by_x(zh, y, 0, x_ref.at[:, lanes_of[0]])
    if pair:
        o_ref[y, zh, x, core] = x_ref[...]
    else:
        o_ref[y, zh, x] = x_ref[...]
    yield
    finish(near_y)
    wide_x = by_x(zh, everything, 1, None)
    finish(near_x)
    wide_y = by_y(zh, everything, 0, None)
    yield
    far = 1 - zh
    arrived(spot(y, far, x, whole), across, device(y, far, x))
    far_y = by_y(far, x, 1, None)
    far_x = by_x(far, y, 0, None)
    yield
    swaps = []
    far_columns = lambda p, of: spot(everything, far, p, lanes_of[1], of)
    far_rows = lambda p, of: spot(p, far, everything, lanes_of[0], of)
    finish(far_y)
    far_wide_x = by_x(far, everything, 1, None)
    finish(far_x)
    far_wide_y = by_y(far, everything, 0, None)
    if pair:
        hand_over(swaps, far_columns, x)
        hand_over(swaps, far_rows, y)
    yield
    finish(wide_x)
    finish(wide_y)

    if pair:
        hand_over(swaps, lambda p, of: o_ref.at[:, p, :, of], zh)
        yield
        finish_and_hand(swaps, far_wide_x, NX, x, far_columns)
        finish_and_hand(swaps, far_wide_y, NY, y, far_rows)
        yield
        finish(swaps)
    else:
        finish(far_wide_x)
        finish(far_wide_y)
    for copy in sent:
        copy.wait_send()


def gather_copies(pair):
    return 1 + 4 * (NX - 1 + NY - 1) + (1 + NX + NY if pair else 0)


def line_places(row, col):
    core = lax.rem(row, 2)
    chip = row // 2
    parity = lax.rem(chip, 2)
    right = (jnp.minimum(row + 4, 2 * CHIPS - 4 + 2 * parity + core), col)
    left = (jnp.maximum(row - 4, 2 * parity + core), col)
    return chip // 2, parity, core, (row + 1 - 2 * core, col), (row + 2 - 4 * parity, col), left, right


def reduce_steps(subs, x_ref, o_ref, acc, near, from_left, from_right, swap, ssem, rsem):
    me, parity, core, partner, mate, left, right = line_places(lax.axis_index("row"), lax.axis_index("col"))
    length = CHIPS // 2
    has_left, has_right = me > 0, me < length - 1
    piece = acc.shape[0] // CHIPS // subs
    mine = lambda b: 2 * b + parity
    others = lambda b: 2 * b + 1 - parity

    def part(j, q):
        return (pl.ds(pl.multiple_of((j * subs + q) * piece, 8), piece), slice(None))

    def copy(source, target, kind, j, q, to):
        return pltpu.make_async_remote_copy(
            src_ref=source,
            dst_ref=target,
            send_sem=ssem.at[kind, j, q],
            recv_sem=rsem.at[kind, j, q],
            device_id=to,
            device_id_type=MESH,
        )

    def here(buffer, kind, to):
        return lambda j, q: copy(buffer.at[part(j, q)], buffer.at[part(j, q)], kind, j, q, to)

    def swap_copy(j, q):
        return copy(x_ref.at[(1 - core,) + part(j, q)], swap.at[part(j, q)], 0, j, q, partner)

    def to_mate(j, q):
        return copy(acc.at[part(j, q)], near.at[part(j, q)], 1, j, q, mate)

    rightward, leftward = here(from_left, 2, right), here(from_right, 3, left)

    def out(kind, to):
        def made(j, q):
            place = o_ref.at[(core,) + part(j, q)]
            return copy(place, place, kind, j, q, to)

        return made

    out_right, out_left, out_mate, out_pair = out(4, right), out(5, left), out(6, mate), out(7, partner)

    def other_pair(j, q):
        there = o_ref.at[(1 - core,) + part(j, q)]
        return copy(there, there, 7, j, q, partner)

    def joined(j, q):
        swap_copy(j, q).wait_recv()
        at = part(j, q)
        return x_ref[(core,) + at] + swap[at]

    def with_mate(j, q):
        value = joined(j, q)
        to_mate(j, q).wait_recv()
        return value + near[part(j, q)]

    order = []
    for k in range(length // 2):
        order += [length - 1 - k, k]
    for b in order:
        for q in range(subs):
            swap_copy(others(b), q).start()
            swap_copy(mine(b), q).start()
    yield
    for b in order:
        for q in range(subs):
            acc[part(others(b), q)] = joined(others(b), q)
            to_mate(others(b), q).start()
    yield

    for s in range(length - 1):
        for q in range(subs):

            @pl.when(jnp.logical_and(me <= s, has_right))
            def _():
                j = mine(me + length - 1 - s)
                at = part(j, q)
                value = with_mate(j, q)

                @pl.when(has_left)
                def _():
                    rightward(j, q).wait_recv()
                    from_left[at] = from_left[at] + value

                @pl.when(jnp.logical_not(has_left))
                def _():
                    from_left[at] = value

                rightward(j, q).start()

            @pl.when(jnp.logical_and(me >= length - 1 - s, has_left))
            def _():
                j = mine(me - (length - 1) + s)
                at = part(j, q)
                value = with_mate(j, q)

                @pl.when(has_right)
                def _():
                    leftward(j, q).wait_recv()
                    from_right[at] = from_right[at] + value

                @pl.when(jnp.logical_not(has_right))
                def _():
                    from_right[at] = value

                leftward(j, q).start()

        yield

    for q in range(subs):
        j = mine(me)
        at = part(j, q)
        acc[at] = with_mate(j, q)

        @pl.when(has_left)
        def _():
            rightward(j, q).wait_recv()
            acc[at] = acc[at] + from_left[at]

        @pl.when(has_right)
        def _():
            leftward(j, q).wait_recv()
            acc[at] = acc[at] + from_right[at]

        o_ref[(core,) + at] = acc[at]

        @pl.when(has_right)
        def _():
            out_right(j, q).start()

        @pl.when(has_left)
        def _():
            out_left(j, q).start()

        out_mate(j, q).start()
        out_pair(j, q).start()

    yield

    def pass_on(b, q):
        out_mate(others(b), q).wait_recv()
        out_pair(others(b), q).start()

    for s in range(1, length + 1):
        for q in range(subs):
            if s < length:

                @pl.when(me >= s)
                def _():
                    j = mine(me - s)
                    out_right(j, q).wait_recv()

                    @pl.when(has_right)
                    def _():
                        out_right(j, q).start()

                    out_mate(j, q).start()
                    out_pair(j, q).start()

                @pl.when(me <= length - 1 - s)
                def _():
                    j = mine(me + s)
                    out_left(j, q).wait_recv()

                    @pl.when(has_left)
                    def _():
                        out_left(j, q).start()

                    out_mate(j, q).start()
                    out_pair(j, q).start()

            if s == 1:
                pass_on(me, q)
            else:

                @pl.when(me >= s - 1)
                def _():
                    pass_on(me - (s - 1), q)

                @pl.when(me <= length - s)
                def _():
                    pass_on(me + (s - 1), q)

        yield

    def finish(b, _):
        for q in range(subs):
            j = mine(b)
            swap_copy(j, q).wait_send()
            swap_copy(others(b), q).wait_send()
            to_mate(others(b), q).wait_send()

            @pl.when(jnp.logical_and(has_right, b > me))
            def _():
                rightward(j, q).wait_send()

            @pl.when(jnp.logical_and(has_left, b < me))
            def _():
                leftward(j, q).wait_send()

            @pl.when(jnp.logical_and(has_right, b <= me))
            def _():
                out_right(j, q).wait_send()

            @pl.when(jnp.logical_and(has_left, b >= me))
            def _():
                out_left(j, q).wait_send()

            out_mate(j, q).wait_send()
            for k in (j, others(b)):
                out_pair(k, q).wait_send()
                other_pair(k, q).wait_recv()
        return 0

    lax.fori_loop(0, length, finish, 0)


def rows_kernel(x_ref, o_ref, ssem, rsem):
    greet(gather_peers(lax.axis_index("row"), lax.axis_index("col")), [])
    for _ in gather_steps(False, x_ref, o_ref, ssem, rsem):
        pass


def short_sum_kernel(x_ref, o_ref, acc, swap, got, ssem, rsem):
    row = lax.axis_index("row")
    col = lax.axis_index("col")
    core = lax.rem(row, 2)
    me = row // 2
    partner = (row + 1 - 2 * core, col)
    on_line = lambda k: (2 * k + core, col)
    ahead = lambda d: lax.rem(me + d, CHIPS)
    behind = lambda d: lax.rem(me + CHIPS - d, CHIPS)
    lanes = acc.shape[1] // CHIPS
    chunk = lambda j: (slice(None), pl.ds(pl.multiple_of(j * lanes, lanes), lanes))
    order = list(range(1, CHIPS))
    greet([partner] + [on_line(ahead(d)) for d in order], [])

    def copy(source, target, number, to):
        return pltpu.make_async_remote_copy(
            src_ref=source,
            dst_ref=target,
            send_sem=ssem.at[number],
            recv_sem=rsem.at[number],
            device_id=to,
            device_id_type=MESH,
        )

    first = copy(x_ref.at[1 - core], swap, 0, partner)
    first.start()
    first.wait_recv()
    acc[...] = x_ref[core] + swap[...]
    inward = [copy(acc.at[chunk(ahead(d))], got.at[me], d, on_line(ahead(d))) for d in order]
    for one in inward:
        one.start()
    total = acc[chunk(me)]
    for d in order:
        there = got.at[behind(d)]
        copy(there, there, d, on_line(behind(d))).wait_recv()
        total = total + got[behind(d)]
    o_ref[chunk(me)] = total
    mine = o_ref.at[chunk(me)]
    outward = [copy(mine, mine, CHIPS - 1 + d, on_line(ahead(d))) for d in order]
    for one in outward:
        one.start()
    for d in order:
        there = o_ref.at[chunk(behind(d))]
        copy(there, there, CHIPS - 1 + d, on_line(behind(d))).wait_recv()
    for one in [first] + inward + outward:
        one.wait_send()


def joint_kernel(subs, g_ref, x_ref, gram_ref, o_ref, acc, near, from_left, from_right, swap, gs, gr, ssem, rsem):
    row = lax.axis_index("row")
    col = lax.axis_index("col")
    me, _, _, partner, mate, left, right = line_places(row, col)
    greet(gather_peers(row, col) + [partner, mate], [(me > 0, left), (me < CHIPS // 2 - 1, right)])
    gather = gather_steps(True, g_ref, gram_ref, gs, gr)
    reduce = reduce_steps(subs, x_ref, o_ref, acc, near, from_left, from_right, swap, ssem, rsem)
    for turn in "grrgrgrrgrrgrrg":
        next(gather if turn == "g" else reduce, None)
    for rest in (reduce, gather):
        for _ in rest:
            pass


def cost(us):
    return pl.CostEstimate(flops=int(us * 1e9), bytes_accessed=int(us * 3e6), transcendentals=0)


def params(collective_id):
    return pltpu.CompilerParams(collective_id=collective_id, has_side_effects=True)


def dma(*shape):
    return pltpu.SemaphoreType.DMA(shape)


def gather_rows(block, collective_id):
    copies = gather_copies(False)
    return pl.pallas_call(
        rows_kernel,
        out_shape=jax.ShapeDtypeStruct((NY, NZH, NX) + block.shape, block.dtype),
        in_specs=[VMEM],
        out_specs=VMEM,
        scratch_shapes=[dma(copies), dma(copies)],
        compiler_params=params(collective_id),
        cost_estimate=cost(35),
        name="gather_rows",
    )(block)


def short_sum(halves, collective_id):
    _, rows, lanes = halves.shape
    half = pltpu.VMEM((rows, lanes), halves.dtype)
    return pl.pallas_call(
        short_sum_kernel,
        out_shape=jax.ShapeDtypeStruct((rows, lanes), halves.dtype),
        in_specs=[VMEM],
        out_specs=VMEM,
        scratch_shapes=[
            half,
            half,
            pltpu.VMEM((CHIPS, rows, lanes // CHIPS), halves.dtype),
            dma(2 * CHIPS - 1),
            dma(2 * CHIPS - 1),
        ],
        compiler_params=params(collective_id),
        cost_estimate=cost(20),
        name="short_sum",
    )(halves)


def joint(gram_half, halves, subs, collective_id):
    _, rows, lanes = halves.shape
    half = pltpu.VMEM((rows, lanes), halves.dtype)
    copies = gather_copies(True)
    return pl.pallas_call(
        functools.partial(joint_kernel, subs),
        out_shape=(
            jax.ShapeDtypeStruct((NY, NZH, NX, 2) + gram_half.shape, gram_half.dtype),
            jax.ShapeDtypeStruct(halves.shape, halves.dtype),
        ),
        in_specs=[VMEM, VMEM],
        out_specs=(VMEM, VMEM),
        scratch_shapes=[half] * 5 + [dma(copies), dma(copies), dma(8, CHIPS, subs), dma(8, CHIPS, subs)],
        compiler_params=params(collective_id),
        cost_estimate=cost(55),
        name="gram_and_sum",
    )(gram_half, halves)


def scaled_inverses(diag_blocks):
    order = diag_blocks.shape[-1]
    at_row = lax.broadcasted_iota(jnp.int32, (order, order), 0)
    at_col = lax.broadcasted_iota(jnp.int32, (order, order), 1)
    halves = 0.5 * jnp.sum(jnp.where(at_row == at_col, diag_blocks, 0.0), axis=2)
    strict = jnp.where(at_row < at_col, -diag_blocks / halves[:, :, None], 0.0)
    size = 16
    power = jnp.where(at_row // size == at_col // size, strict, 0.0)
    inverse = jnp.where(at_row == at_col, 1.0, power)
    for _ in range(3):
        power = matmul(power, power)
        inverse = inverse + matmul(inverse, power)
    while size < order:
        corner = jnp.where(
            jnp.logical_and(at_row // (2 * size) == at_col // (2 * size), at_row // size != at_col // size), strict, 0.0
        )
        inverse = inverse + matmul(matmul(inverse, corner), inverse)
        size *= 2
    return inverse, 1.0 / halves


def solve_turned(gram, product):
    order = gram.shape[0] // PANELS
    cut = lambda p: slice(p * order, (p + 1) * order)
    inverse, scale = scaled_inverses(jnp.stack([gram[cut(p), cut(p)] for p in range(PANELS)]))
    done = None
    for p in reversed(range(PANELS)):
        rest = product[:, cut(p)]
        if done is not None:
            rest = rest - contract(done, gram[cut(p), (p + 1) * order :], 1, 1)
        here = contract(rest * scale[p][None, :], inverse[p], 1, 1)
        done = here if done is None else jnp.concatenate([here, done], axis=1)
    return done


def permute_blocks(spread, owner_list, slot_list):
    blocks = owner_list.shape[0]
    target = owner_list * BLK_DEV + slot_list
    positions = jnp.arange(blocks, dtype=jnp.int32)
    one_hot = (target[:, None] == positions[None, :]).astype(jnp.float32)
    ordered = jnp.einsum(
        "rbw,bc->rcw",
        spread.reshape(spread.shape[0], blocks, BW),
        one_hot,
        precision=lax.Precision.HIGHEST,
        preferred_element_type=jnp.float32,
    )
    return ordered.reshape(spread.shape[0], blocks * BW)


def on_device(vectors, reflectors, owner_list, slot_list):
    panels, rows, width = reflectors.shape
    order = panels * width
    col = lax.axis_index("col")
    spread = lax.all_to_all(vectors, "col", split_axis=0, concat_axis=1, tiled=True)
    own_rows = jnp.transpose(reflectors, (1, 0, 2)).reshape(rows, order)
    panel_rows = gather_rows(own_rows, 0).reshape(NY * NZH * NX * rows, order)
    ordered = permute_blocks(spread, owner_list, slot_list)
    panel_rows, ordered = lax.optimization_barrier((panel_rows, ordered))
    slab_now = lax.all_to_all(ordered, "col", split_axis=1, concat_axis=0, tiled=True)
    share = order // (NY * NZH * NX)
    own_columns = lax.dynamic_slice_in_dim(panel_rows, col * share, share, axis=1)
    gram_part = contract(own_columns, panel_rows, 0, 0, lax.Precision.HIGHEST)
    gram_half = short_sum(gram_part.reshape(2, share // 2, order), 1)
    product_part = contract(slab_now, panel_rows, 0, 0)
    columns = product_part.shape[0]
    gram, product = joint(gram_half, product_part.reshape(2, columns // 2, order), 2, 2)
    turned = solve_turned(gram.reshape(order, order), product.reshape(columns, order))
    return slab_now - contract(panel_rows, turned, 1, 1)


def solution(mesh):
    return jax.shard_map(
        on_device,
        mesh=mesh,
        in_specs=(P("row", "col"), P(None, ("row", "col"), None), P(), P()),
        out_specs=P("row", "col"),
        check_vma=False,
    )
```
